768 devices in a mesh: fsdp: 48 (over z, y_lo), seq: 16 (over y_hi, x, core).
Axes of the slice: x: 4, y: 8 (y_hi: 2, y_lo: 4; y = y_hi * 4 + y_lo), z: 12, core: 2. Of those that a mesh axis runs over, the one named last changes fastest.
Arguments:
- tokens: bfloat16 [48, 2048, 2304], P('fsdp', 'seq'), may hold values from -6 to 6
- queries: bfloat16 [48, 2048, 2048], P('fsdp', 'seq'), may hold values from -9 to 9
- key_rows: bfloat16 [48, 2048, 512], P('fsdp', 'seq'), may hold values from -9 to 9
- out_grad: bfloat16 [48, 2048, 2048], P('fsdp', 'seq'), may hold values from -0.0625 to 0.0625
- value_weight: bfloat16 [2304, 512], P('fsdp'), may hold values from -0.125 to 0.125
- documents: int32 [48, 2048], P('fsdp'), may hold values from 0 to 15, never falling along the last dimension, each value on 1 to 512 neighbouring positions
- block_plan: int32 [48, 16], P('fsdp'), may hold values from 0 to 15, each once within a row
Outputs:
- attended: bfloat16 [48, 2048, 2048], P('fsdp', 'seq')
- weight_grad: float32 [2304, 512], P(('fsdp', 'seq'))
The draws below stay inside these ranges and needn't reach their ends.
Inputs may be any that keep to these rules, and one draw needn't show every extreme that they name: `documents`: document numbers never fall along a sequence; each document covers at most 512 places, and one covers exactly that many. `block_plan`: each row names every block of its sequence once.
All inputs are finite; a program needn't handle non-finite values.
Results may differ from the reference program's by a relative error of at most 0.018.
Values may be sent and summed in bfloat16 or wider, within the bound.
A program may use at most 32 MiB of HBM per device.

```python
import math
import jax
import jax.numpy as jnp
import numpy as np
from jax import lax

TOK_DEV = 128
DW = 2304
QH = 16
KH = 4
HD = 128
BLOCK = 128
SEQS = 48
LEN = 2048
NBLK = 16
DOCS = 16
N_SEQ = 16


def draw_queries(key, part):
    noise_key = jax.random.fold_in(key, 11)
    values = jnp.clip(jax.random.normal(noise_key, (SEQS, LEN, QH * HD), jnp.float32), -6.0, 6.0)
    return values.astype(jnp.bfloat16)


def draw_key_rows(key, part):
    noise_key = jax.random.fold_in(key, 23)
    values = jnp.clip(jax.random.normal(noise_key, (SEQS, LEN, KH * HD), jnp.float32), -6.0, 6.0)
    return values.astype(jnp.bfloat16)


def spiked(array, rng, source, target, shards_of, factor):
    def block_of(dim):
        return (jnp.arange(array.shape[dim]) // (array.shape[dim] // shards_of)).reshape((-1,) + (1,) * (array.ndim - 1 - dim))

    one_side = jax.random.permutation(rng, shards_of)[block_of(target)]
    other_side = (block_of(target) + shards_of // 2) % shards_of
    return jnp.where((block_of(source) == one_side) | (block_of(source) == other_side), factor * array, array)


def shard_levels(stream_key, extent, cuts, smallest, high):
    gain, own = 1.0, jax.random.fold_in(stream_key, 6)
    for position, blocks in cuts:
        steps = jnp.exp(jax.random.uniform(jax.random.fold_in(own, position), (blocks,), jnp.float32, smallest / len(cuts), high / len(cuts)))
        gain = gain * jnp.repeat(steps, extent[position] // blocks).reshape([-1 if axis == position else 1 for axis in range(len(extent))])
    return gain


def profile(number_of, total, most, slope):
    weights = [(1 << 20) // math.isqrt(grade ** slope) + 1 for grade in range(2, number_of + 1)]
    rest, holding = total - most - (number_of - 1), [1] * (number_of - 1)
    while rest > 0:
        candidates = [i for i in range(number_of - 1) if holding[i] < most]
        whole, budget = sum([weights[i] for i in candidates]), rest
        for i in candidates:
            extra = min(most - holding[i], max(1, budget * weights[i] // whole), rest)
            holding[i] = holding[i] + extra
            rest = rest - extra
    return np.array([most] + holding)


def uneven_parts(key, count, total, most, slope):
    if count == 2:
        one = jax.random.randint(key, (), max(1, total - most), min(most, total - 1) + 1)
        return jnp.stack([one, total - one])
    sizes = jnp.asarray(profile(count, total, most, slope), jnp.int32)
    couples = (count - 1) // 2
    donor, taker = sizes[1:1 + 2 * couples:2], sizes[2:2 + 2 * couples:2]
    margin = jnp.minimum(donor - 1, most - taker)
    passed = jax.random.randint(jax.random.fold_in(key, 1), (couples,), 0, 1 << 20) % (margin + 1)
    sizes = sizes.at[1:1 + 2 * couples:2].set(donor - passed).at[2:2 + 2 * couples:2].set(taker + passed)
    return sizes[jax.random.permutation(jax.random.fold_in(key, 2), count)]


def bell_draw(stream_key, shape, scale, most, shards=(), held_as=jnp.bfloat16):
    array = scale * jax.random.normal(stream_key, shape, jnp.float32)
    if shards:
        array = array * shard_levels(stream_key, shape, shards, -0.22, 0.18)
    return jnp.clip(array, -most, most).astype(held_as)


def bell_draw_with(stream_key, extent, scale, limit, cuts, heavy, held_as=jnp.bfloat16):
    values = scale * jax.random.normal(stream_key, extent, jnp.float32)
    if cuts:
        values = values * shard_levels(stream_key, extent, cuts, -0.22, 0.18)
    return jnp.clip(spiked(values, jax.random.fold_in(stream_key, 3), *heavy), -limit, limit).astype(held_as)


def setup_inputs(seed: int = 0) -> dict:
    seeds = jax.random.split(jax.random.key(seed), 8)
    tokens = bell_draw_with(seeds[0], (SEQS, LEN, DW), 1.0, 6.0, ((0, 48), (1, 16)), (0, 2, 48, 3.25))
    queries = draw_queries(jax.random.fold_in(seeds[7], 71), 0)
    key_rows = draw_key_rows(jax.random.fold_in(seeds[7], 71), 0)
    out_grad = bell_draw(seeds[3], (SEQS, LEN, QH * HD), 0.004, 0.0625, ((0, 48), (1, 16)))
    value_weight = bell_draw(seeds[4], (DW, KH * HD), DW ** -0.5, 0.125, ((0, 48),))
    documents = jax.vmap(lambda own: jnp.searchsorted(jnp.cumsum(uneven_parts(own, DOCS, LEN, LEN // 4, 2)), jnp.arange(LEN), side="right"))(jax.random.split(seeds[5], SEQS)).reshape((SEQS, LEN)).astype(jnp.int32)
    block_plan = jax.vmap(lambda own: jax.random.permutation(own, NBLK))(jax.random.split(seeds[6], SEQS)).reshape((SEQS, NBLK)).astype(jnp.int32)
    return {"tokens": tokens, "queries": queries, "key_rows": key_rows, "out_grad": out_grad, "value_weight": value_weight, "documents": documents, "block_plan": block_plan}


def attend_group(visible, group_query, group_key, group_value, group_grad):
    scores = jnp.einsum('hqd,kd->hqk', group_query.astype(jnp.float32), group_key.astype(jnp.float32)) * (HD ** -0.5)
    scores = jnp.where(visible[None], scores, -jnp.inf)
    row_max = jnp.max(scores, axis=2, keepdims=True)
    exponent = jnp.exp(scores - row_max)
    weights = (exponent / jnp.sum(exponent, axis=2, keepdims=True)).astype(jnp.bfloat16)
    outputs = jnp.einsum('hqk,kd->hqd', weights.astype(jnp.float32), group_value.astype(jnp.float32)).astype(jnp.bfloat16)
    head_grads = jnp.einsum('hqk,hqd->hkd', weights.astype(jnp.float32), group_grad.astype(jnp.float32)).astype(jnp.bfloat16)
    group_total = jnp.sum(head_grads.astype(jnp.float32), axis=0).astype(jnp.bfloat16)
    return outputs, group_total


def one_sequence(inputs):
    queries, key_rows, values, out_grad, positions, segment_ids = inputs
    length = positions.shape[0]
    group_size = QH // KH
    visible = (segment_ids[:, None] == segment_ids[None, :]) & (positions[None, :] <= positions[:, None])
    query_groups = queries.reshape(length, KH, group_size, HD).transpose(1, 2, 0, 3)
    grad_groups = out_grad.reshape(length, KH, group_size, HD).transpose(1, 2, 0, 3)
    key_groups = key_rows.reshape(length, KH, HD).transpose(1, 0, 2)
    value_groups = values.reshape(length, KH, HD).transpose(1, 0, 2)
    outputs, group_grads = lax.map(
        lambda group_item: attend_group(visible, group_item[0], group_item[1], group_item[2], group_item[3]),
        (query_groups, key_groups, value_groups, grad_groups))
    attended = outputs.transpose(2, 0, 1, 3).reshape(length, QH * HD)
    value_grad = group_grads.transpose(1, 0, 2).reshape(length, KH * HD)
    return attended, value_grad


def reference(tokens, queries, key_rows, out_grad, value_weight, documents, block_plan):
    sequences, length, features = tokens.shape
    columns = value_weight.shape[1]
    values = jnp.dot(tokens.reshape(sequences * length, features), value_weight,
                     preferred_element_type=jnp.float32).astype(jnp.bfloat16).reshape(sequences, length, columns)
    offsets = jnp.arange(BLOCK, dtype=jnp.int32)
    positions = (block_plan[:, :, None] * BLOCK + offsets[None, None, :]).reshape(sequences, length).astype(jnp.int32)
    segment_ids = jnp.take_along_axis(documents, positions, axis=1)
    attended, value_grad = lax.map(one_sequence, (queries, key_rows, values, out_grad, positions, segment_ids))
    token_blocks = tokens.reshape(sequences, N_SEQ, TOK_DEV, features)
    grad_blocks = value_grad.reshape(sequences, N_SEQ, TOK_DEV, columns)

    def accumulate(running, blocks_pair):
        term_set = jnp.einsum('std,stc->sdc', blocks_pair[0].astype(jnp.float32), blocks_pair[1].astype(jnp.float32)).astype(jnp.bfloat16)
        term_set = lax.optimization_barrier(term_set).astype(jnp.float32)
        return running + jnp.sum(term_set, axis=0), None

    weight_grad, unused = lax.scan(accumulate, jnp.zeros((features, columns), jnp.float32), (token_blocks, grad_blocks))
    return attended, weight_grad
```

```python
import jax
import jax.numpy as jnp
from jax import lax
from jax.experimental import pallas as pl
from jax.experimental.pallas import tpu as pltpu
from jax.sharding import PartitionSpec as P

BLOCK = 128
HD = 128
GROUP = 4
NX, NY, NZ, NYL = 4, 8, 12, 4
BF16 = jnp.bfloat16
F32 = jnp.float32
MESH = pl.DeviceIdType.MESH


def body(
    tok_hbm, q_hbm, k_hbm, do_hbm, w_hbm, docs_ref, plan_ref,
    att_out, wg_out,
    tok2, q2, do2, kall, vall, wbuf, bias, wts, slots, dvs, dvr, dvt, vgp, att2,
    gs, gr, ysum, xf, xs, xr, xsum, zs, zr, cs, cr,
    lsem, es, er, wys, wyr, wzs, wzr, ks, kr, vs, vr, ds_, dr, gys, gyr, xss, xrs, zss, zrs,
):
    f = lax.axis_index("fsdp")
    s = lax.axis_index("seq")
    z, yl = f // NYL, f % NYL
    yh, x, c = s // 8, (s // 2) % NX, s % 2
    y = yh * NYL + yl
    chip = s // 2

    def dev(z_, y_, x_, c_):
        return (z_ * NYL + y_ % NYL, (y_ // NYL) * 8 + x_ * 2 + c_)

    xp, xm, x2 = (x + 1) % NX, (x + 3) % NX, (x + 2) % NX
    core_dev = dev(z, y, x, 1 - c)
    xp_dev, xm_dev, x2_dev = dev(z, y, xp, c), dev(z, y, xm, c), dev(z, y, x2, c)
    yp_dev, ym_dev = dev(z, (y + 1) % NY, x, c), dev(z, (y + 7) % NY, x, c)
    yp2_dev, ym2_dev = dev(z, (y + 2) % NY, x, c), dev(z, (y + 6) % NY, x, c)
    y4_dev = dev(z, (y + 4) % NY, x, c)
    zp_dev, zm_dev = dev((z + 1) % NZ, y, x, c), dev((z + 11) % NZ, y, x, c)

    barrier = pltpu.get_barrier_semaphore()
    near = [core_dev, xp_dev, xm_dev, x2_dev, yp_dev, ym_dev, yp2_dev, ym2_dev, y4_dev]
    for d in range(1, NZ):
        pl.semaphore_signal(barrier, inc=1, device_id=dev((z + d) % NZ, y, x, c), device_id_type=MESH)
    for target in near:
        pl.semaphore_signal(barrier, inc=1, device_id=target, device_id_type=MESH)
    pl.semaphore_wait(barrier, len(near) + NZ - 1)

    def remote(src, dst, ssem, rsem, target):
        return pltpu.make_async_remote_copy(
            src_ref=src, dst_ref=dst, send_sem=ssem, recv_sem=rsem,
            device_id=target, device_id_type=MESH,
        )

    started = []

    def send(src, dst, ssem, rsem, target):
        copy = remote(src, dst, ssem, rsem, target)
        copy.start()
        started.append(copy)
        return copy

    col = pl.ds(pl.multiple_of(c * 256, 256), 256)
    other_col = pl.ds(pl.multiple_of((1 - c) * 256, 256), 256)
    wide = pl.ds(pl.multiple_of(c * 1024, 1024), 1024)
    other_wide = pl.ds(pl.multiple_of((1 - c) * 1024, 1024), 1024)

    ek = send(k_hbm.at[:, other_col], kall.at[s], es.at[0], er.at[0], core_dev)
    lk = pltpu.make_async_copy(k_hbm.at[:, col], kall.at[s], lsem.at[0])
    lk.start()
    w_own = w_hbm.at[:, col]
    wy = [
        None,
        send(w_own, wbuf.at[f], wys.at[1], wyr.at[1], ym_dev),
        send(w_own, wbuf.at[f], wys.at[2], wyr.at[2], yp2_dev),
        send(w_own, wbuf.at[f], wys.at[3], wyr.at[3], yp_dev),
    ]
    lw = pltpu.make_async_copy(w_own, wbuf.at[f], lsem.at[1])
    lw.start()

    def ring_copies(t, i):
        cls = (yl + i) % NYL
        plus = ((z + NZ - (t - 1)) % NZ) * NYL + cls
        out = [remote(wbuf.at[plus], wbuf.at[plus], wzs.at[0, t - 1, i], wzr.at[0, t - 1, i], zp_dev)]
        minus = ((z + t - 1) % NZ) * NYL + cls
        out.append(remote(wbuf.at[minus], wbuf.at[minus], wzs.at[1, t - 1, i], wzr.at[1, t - 1, i], zm_dev))
        return out

    z_first = [
        send(w_own, wbuf.at[f], wzs.at[0, 0, 0], wzr.at[0, 0, 0], zp_dev),
        send(w_own, wbuf.at[f], wzs.at[1, 0, 0], wzr.at[1, 0, 0], zm_dev),
    ]
    eq = send(q_hbm.at[:, other_wide], q2.at[c], es.at[1], er.at[1], core_dev)
    lq = pltpu.make_async_copy(q_hbm.at[:, wide], q2.at[c], lsem.at[2])
    lq.start()
    ed = send(do_hbm.at[:, other_wide], do2.at[c], es.at[2], er.at[2], core_dev)
    ld = pltpu.make_async_copy(do_hbm.at[:, wide], do2.at[c], lsem.at[3])
    ld.start()
    et = send(tok_hbm, tok2.at[c], es.at[3], er.at[3], core_dev)
    lt = pltpu.make_async_copy(tok_hbm, tok2.at[c], lsem.at[4])
    lt.start()

    def gather_start(buf, ss, rs):
        own = buf.at[pl.ds(2 * chip, 2)]
        return [
            send(own, own, ss.at[0], rs.at[0], y4_dev),
            send(own, own, ss.at[1], rs.at[1], xp_dev),
            send(own, own, ss.at[2], rs.at[2], xm_dev),
        ]

    def gather_own_forward(buf, ss, rs, first):
        first[1].wait_recv()
        a = buf.at[2 * (yh * NX + xm)]
        up = send(a, a, ss.at[5], rs.at[5], xp_dev)
        first[2].wait_recv()
        b = buf.at[2 * (yh * NX + xp) + 1]
        down = send(b, b, ss.at[6], rs.at[6], xm_dev)
        return [up, down]

    def gather_peer(buf, ss, rs, first):
        first[0].wait_recv()
        peer = buf.at[pl.ds(2 * ((1 - yh) * NX + x), 2)]
        return [
            send(peer, peer, ss.at[3], rs.at[3], xp_dev),
            send(peer, peer, ss.at[4], rs.at[4], xm_dev),
        ]

    def gather_peer_forward(buf, ss, rs, second):
        second[0].wait_recv()
        a = buf.at[2 * ((1 - yh) * NX + xm)]
        up = send(a, a, ss.at[7], rs.at[7], xp_dev)
        second[1].wait_recv()
        b = buf.at[2 * ((1 - yh) * NX + xp) + 1]
        down = send(b, b, ss.at[8], rs.at[8], xm_dev)
        return [up, down]

    lk.wait()
    ek.wait_recv()
    k_first = gather_start(kall, ks, kr)
    for i in (1, 3, 2):
        wy[i].wait_recv()
        for copy in ring_copies(1, i):
            copy.start()
            started.append(copy)

    def ring_step(t):
        for i in (0, 1, 3, 2):
            before = ring_copies(t - 1, i)
            after = ring_copies(t, i)
            before[0].wait_recv()
            after[0].start()
            started.append(after[0])
            before[1].wait_recv()
            if t <= 5:
                after[1].start()
                started.append(after[1])

    k_own = gather_own_forward(kall, ks, kr, k_first)
    ring_step(2)

    places = [plan_ref[0, 2 * chip + b] for b in range(2)]
    key_at = []
    row_i = lax.broadcasted_iota(jnp.int32, (BLOCK, BLOCK), 0)
    col_i = lax.broadcasted_iota(jnp.int32, (BLOCK, BLOCK), 1)
    for b in range(2):
        rows = docs_ref[pl.ds(places[b], 1), :].astype(F32)
        ats = []
        for j in range(5):
            place = places[b] - j
            at = jnp.int32(0)
            for t in range(16):
                at = jnp.where(plan_ref[0, t] == place, t, at)
            ats.append(at)
            keys = docs_ref[pl.ds(jnp.maximum(place, 0), 1), :].astype(F32)
            keys = jnp.where(place >= 0, keys, jnp.float32(-1.0))
            keys = jnp.broadcast_to(keys, (BLOCK, BLOCK))
            column = jnp.sum(jnp.where(row_i == col_i, keys, 0.0), axis=1, keepdims=True)
            seen = jnp.broadcast_to(column, (BLOCK, BLOCK)) == jnp.broadcast_to(rows, (BLOCK, BLOCK))
            if j == 0:
                seen = seen & (row_i <= col_i)
            bias[b, pl.ds(j * BLOCK, BLOCK), :] = jnp.where(seen, jnp.float32(0.0), jnp.float32(-jnp.inf))
        key_at.append(ats)

    k_second = gather_peer(kall, ks, kr, k_first)
    ring_step(3)
    k_third = gather_peer_forward(kall, ks, kr, k_second)
    lq.wait()
    eq.wait_recv()
    ld.wait()
    ed.wait_recv()
    ring_step(4)
    for copy in k_own + k_third:
        copy.wait_recv()

    def weigh(b):
        def group(g, carry):
            lanes = pl.ds(pl.multiple_of(g * HD, HD), HD)
            keys = jnp.concatenate([kall[at, :, lanes] for at in key_at[b]], axis=0)
            total = jnp.zeros((5 * BLOCK, HD), F32)
            for h in range(GROUP):
                head = pl.ds(pl.multiple_of((g * GROUP + h) * HD, HD), HD)
                scores = lax.dot_general(
                    keys, q2[b, :, head], (((1,), (1,)), ((), ())), preferred_element_type=F32
                ) * F32(HD ** -0.5) + bias[b]
                peak = jnp.max(scores, axis=0, keepdims=True)
                exponent = jnp.exp(scores - peak)
                inverse = 1.0 / jnp.sum(exponent, axis=0, keepdims=True)
                weights = (exponent * inverse).astype(BF16)
                wts[b, g * GROUP + h] = weights
                total = total + jnp.dot(weights, do2[b, :, head], preferred_element_type=F32)
            for j in range(5):
                slots[b, j, :, lanes] = total[j * BLOCK:(j + 1) * BLOCK]
            return carry

        lax.fori_loop(0, 2, group, 0)
        slots[b, 5] = jnp.zeros((BLOCK, 256), F32)

    weigh(0)
    ring_step(5)
    weigh(1)

    def lay(t, carry):
        place = plan_ref[0, t]
        parts = []
        for b in range(2):
            j = places[b] - place
            j = jnp.where((j >= 0) & (j <= 4), j, 5)
            parts.append(slots[b, j])
        dvs[t // 8, (t // 2) % NX, t % 2] = (parts[0] + parts[1]).astype(BF16)
        return carry

    lax.fori_loop(0, 16, lay, 0)

    da = send(dvs.at[:, x2, 0], dvr.at[0], ds_.at[0], dr.at[0], xp_dev)
    db = send(dvs.at[:, x2, 1], dvr.at[1], ds_.at[1], dr.at[1], xm_dev)
    dc = send(dvs.at[:, xp, 1], dvr.at[2], ds_.at[2], dr.at[2], xp_dev)
    dd = send(dvs.at[:, xm, 0], dvr.at[3], ds_.at[3], dr.at[3], xm_dev)

    ring_step(6)
    lt.wait()
    et.wait_recv()
    lw.wait()
    for i in range(NYL):
        ring_copies(6, i)[0].wait_recv()
    weight = wbuf[...].reshape(48 * 48, 256)
    for b in range(2):
        vall[2 * chip + b] = jnp.dot(tok2[b], weight, preferred_element_type=F32).astype(BF16)

    def add_pair(dst, a, b):
        dst[...] = (a[...].astype(F32) + b[...].astype(F32)).astype(BF16)

    da.wait_recv()
    for k in range(2):
        dvt[0, k] = (dvs[k, xp, 0].astype(F32) + dvr[0, k].astype(F32)).astype(BF16)
    de = send(dvt.at[0], dvr.at[4], ds_.at[4], dr.at[4], xp_dev)
    db.wait_recv()
    for k in range(2):
        dvt[1, k] = (dvs[k, xm, 1].astype(F32) + dvr[1, k].astype(F32)).astype(BF16)
    df = send(dvt.at[1], dvr.at[5], ds_.at[5], dr.at[5], xm_dev)
    v_first = gather_start(vall, vs, vr)
    dc.wait_recv()
    dd.wait_recv()
    de.wait_recv()
    df.wait_recv()

    def chip_total(k, b):
        one, two = (3, 4) if b == 0 else (2, 5)
        return dvs[k, x, b].astype(F32) + dvr[one, k].astype(F32) + dvr[two, k].astype(F32)

    for b in range(2):
        vgp[0, b] = chip_total(1 - yh, b).astype(BF16)
    dy = send(vgp.at[0], vgp.at[1], ds_.at[6], dr.at[6], y4_dev)
    v_own = gather_own_forward(vall, vs, vr, v_first)
    dy.wait_recv()
    value_grad = [
        (chip_total(yh, b) + vgp[1, b].astype(F32)).astype(BF16) for b in range(2)
    ]

    for j in range(6):
        lanes = pl.ds(j * 384, 384)
        product = jnp.zeros((384, 256), F32)
        for b in range(2):
            product = product + lax.dot_general(
                tok2[b, :, lanes], value_grad[b], (((0,), (0,)), ((), ())), preferred_element_type=F32
            )
        for a in range(NYL):
            for h in range(2):
                at = (a * 2 + h) * 24
                pair = jnp.concatenate([product[at:at + 24], product[192 + at:192 + at + 24]], axis=0)
                gs[h * NYL + a, pl.ds(j * 48, 48), :] = pair.astype(BF16)

    halves = (pl.ds(0, 144), pl.ds(144, 144))
    streams = ((0, 0, 4), (1, 1, 4), (0, 1, 3), (1, 0, 3))
    y_dev = (yp_dev, ym_dev)

    def y_dest(direction, distance):
        return (y + distance) % NY if direction == 0 else (y + NY - distance) % NY

    def y_copy(stream, hop):
        direction, half, hops = streams[stream]
        at = y_dest(direction, hops - hop)
        return remote(
            gs.at[at, halves[half]], gr.at[stream, hop], gys.at[stream, hop], gyr.at[stream, hop], y_dev[direction]
        )

    flying = []
    for stream in range(4):
        copy = y_copy(stream, 0)
        copy.start()
        started.append(copy)
        flying.append(copy)
    for hop in range(1, 4):
        for stream in range(4):
            direction, half, hops = streams[stream]
            if hop >= hops:
                continue
            flying[stream].wait_recv()
            at = y_dest(direction, hops - hop)
            gs[at, halves[half], :] = (
                gs[at, halves[half], :].astype(F32) + gr[stream, hop - 1].astype(F32)
            ).astype(BF16)
            copy = y_copy(stream, hop)
            copy.start()
            started.append(copy)
            flying[stream] = copy
    v_second = gather_peer(vall, vs, vr, v_first)
    v_third = gather_peer_forward(vall, vs, vr, v_second)
    for stream in range(4):
        flying[stream].wait_recv()
    for half in range(2):
        ysum[halves[half], :] = (
            gs[y, halves[half], :].astype(F32)
            + gr[0 if half == 0 else 2, 3 if half == 0 else 2].astype(F32)
            + gr[3 if half == 0 else 1, 2 if half == 0 else 3].astype(F32)
        )

    for k in range(NX):
        for j in range(NZ):
            xf[k, pl.ds(j * 6, 6), :] = ysum[pl.ds(j * 24 + k * 6, 6), :]
    for k in range(NX):
        xs[k] = xf[k].astype(BF16)
    x_copies = [
        send(xs.at[xp], xr.at[0], xss.at[0], xrs.at[0], xp_dev),
        send(xs.at[xm], xr.at[1], xss.at[1], xrs.at[1], xm_dev),
        send(xs.at[x2], xr.at[2], xss.at[2], xrs.at[2], x2_dev),
    ]

    for copy in v_own + v_third:
        copy.wait_recv()

    def attend(b):
        def group(g, carry):
            lanes = pl.ds(pl.multiple_of(g * HD, HD), HD)
            held = jnp.concatenate([vall[at, :, lanes] for at in key_at[b]], axis=0)
            for h in range(GROUP):
                head = pl.ds(pl.multiple_of((g * GROUP + h) * HD, HD), HD)
                flipped = lax.dot_general(
                    held, wts[b, g * GROUP + h], (((0,), (0,)), ((), ())), preferred_element_type=F32
                )
                att2[b, :, head] = flipped.T.astype(BF16)
            return carry

        lax.fori_loop(0, 2, group, 0)

    for copy in x_copies:
        copy.wait_recv()
    xsum[...] = xf[x] + xr[0].astype(F32) + xr[1].astype(F32) + xr[2].astype(F32)

    zs[...] = jnp.zeros((NZ, 8, 256), F32)
    for j in range(NZ):
        zs[j, 0:6, :] = xsum[pl.ds(j * 6, 6), :]

    z_copies = []
    for d in range(1, NZ):
        there = (z + d) % NZ
        z_copies.append(send(zs.at[there], zr.at[d], zss.at[d], zrs.at[d], dev(there, y, x, c)))
    attend(0)
    attend(1)
    la = pltpu.make_async_copy(att2.at[c], att_out.at[:, wide], lsem.at[5])
    la.start()
    ea = send(att2.at[1 - c], att_out.at[:, wide], es.at[4], er.at[4], core_dev)
    total = zs[z]
    for d in range(1, NZ):
        z_copies[d - 1].wait_recv()
        total = total + zr[d]
    cs[...] = jnp.zeros((2, 8, 256), F32)
    cs[0, 0:3, :] = total[0:3]
    cs[1, 0:3, :] = total[3:6]
    ec = send(cs.at[1 - c], cr, es.at[5], er.at[5], core_dev)
    ec.wait_recv()
    mine, theirs = cs[c], cr[...]
    wg_out[:, 0:256] = jnp.where(c == 0, mine, theirs)[0:3]
    wg_out[:, 256:512] = jnp.where(c == 0, theirs, mine)[0:3]
    la.wait()
    ea.wait_recv()
    for copy in started:
        copy.wait_send()


def shards(tokens, queries, key_rows, out_grad, value_weight, documents, block_plan):
    anywhere = pl.BlockSpec(memory_space=pl.ANY)
    in_vmem = pl.BlockSpec(memory_space=pltpu.VMEM)
    dma = pltpu.SemaphoreType.DMA
    vmem = pltpu.VMEM
    attended, weight_grad = pl.pallas_call(
        body,
        out_shape=(
            jax.ShapeDtypeStruct((BLOCK, 2048), BF16),
            jax.ShapeDtypeStruct((3, 512), F32),
        ),
        in_specs=[anywhere] * 5 + [in_vmem, pl.BlockSpec(memory_space=pltpu.SMEM)],
        out_specs=(anywhere, in_vmem),
        scratch_shapes=[
            vmem((2, BLOCK, 2304), BF16),
            vmem((2, BLOCK, 1024), BF16),
            vmem((2, BLOCK, 1024), BF16),
            vmem((16, BLOCK, 256), BF16),
            vmem((16, BLOCK, 256), BF16),
            vmem((48, 48, 256), BF16),
            vmem((2, 5 * BLOCK, BLOCK), F32),
            vmem((2, 8, 5 * BLOCK, BLOCK), BF16),
            vmem((2, 6, BLOCK, 256), F32),
            vmem((2, NX, 2, BLOCK, 256), BF16),
            vmem((6, 2, BLOCK, 256), BF16),
            vmem((2, 2, BLOCK, 256), BF16),
            vmem((2, 2, BLOCK, 256), BF16),
            vmem((2, BLOCK, 1024), BF16),
            vmem((NY, 288, 256), BF16),
            vmem((4, 4, 144, 256), BF16),
            vmem((288, 256), F32),
            vmem((NX, 72, 256), F32),
            vmem((NX, 72, 256), BF16),
            vmem((3, 72, 256), BF16),
            vmem((72, 256), F32),
            vmem((NZ, 8, 256), F32),
            vmem((NZ, 8, 256), F32),
            vmem((2, 8, 256), F32),
            vmem((8, 256), F32),
            dma((6,)),
            dma((6,)), dma((6,)),
            dma((4,)), dma((4,)),
            dma((2, 6, 4)), dma((2, 6, 4)),
            dma((9,)), dma((9,)),
            dma((9,)), dma((9,)),
            dma((7,)), dma((7,)),
            dma((4, 4)), dma((4, 4)),
            dma((3,)), dma((3,)),
            dma((NZ,)), dma((NZ,)),
        ],
        compiler_params=pltpu.CompilerParams(
            collective_id=0, has_side_effects=True, vmem_limit_bytes=60 * 1024 * 1024
        ),
        name="value_path",
    )(
        tokens[0], queries[0], key_rows[0], out_grad[0], value_weight,
        documents.reshape(16, BLOCK), block_plan,
    )
    return attended[None], weight_grad


def solution(mesh):
    in_specs = (
        P("fsdp", "seq", None),
        P("fsdp", "seq", None),
        P("fsdp", "seq", None),
        P("fsdp", "seq", None),
        P("fsdp", None),
        P("fsdp", None),
        P("fsdp", None),
    )
    out_specs = (P("fsdp", "seq", None), P(("fsdp", "seq"), None))
    return jax.shard_map(shards, mesh=mesh, in_specs=in_specs, out_specs=out_specs, check_vma=False)
```

```python
import jax
import jax.numpy as jnp
from jax import lax
from jax.experimental import pallas as pl
from jax.experimental.pallas import tpu as pltpu
from jax.sharding import PartitionSpec as P

BLOCK = 128
HD = 128
GROUP = 4
NX, NY, NZ, NYL = 4, 8, 12, 4
LOG2E = 1.4426950408889634
BF16 = jnp.bfloat16
F32 = jnp.float32
MESH = pl.DeviceIdType.MESH


def body(
    tok_hbm, q_hbm, k_hbm, do_hbm, w_hbm, docs_ref, plan_ref,
    att_out, wg_out,
    tok2, q2, do2, kall, vall, wbuf, bias, wts, slots, dvs, dvr, dvt, vgp, att2,
    gs, gr, ysum, xf, xs, xr, xsum, gb, xb, xbs, xbr, xbt, yb, ybs, ybr, bsum, zs, zr,
    lsem, es, er, wys, wyr, wzs, wzr, ks, kr, vs, vr, ds_, dr, dys, dyr, gys, gyr, xss, xrs, bs, br, bys, byr, zss, zrs,
):
    f = lax.axis_index("fsdp")
    s = lax.axis_index("seq")
    z, yl = f // NYL, f % NYL
    yh, x, c = s // 8, (s // 2) % NX, s % 2
    y = yh * NYL + yl
    chip = s // 2

    def dev(z_, y_, x_, c_):
        return (z_ * NYL + y_ % NYL, (y_ // NYL) * 8 + x_ * 2 + c_)

    xp, xm, x2 = (x + 1) % NX, (x + 3) % NX, (x + 2) % NX
    core_dev = dev(z, y, x, 1 - c)
    xp_dev, xm_dev, x2_dev = dev(z, y, xp, c), dev(z, y, xm, c), dev(z, y, x2, c)
    yp_dev, ym_dev = dev(z, (y + 1) % NY, x, c), dev(z, (y + 7) % NY, x, c)
    yp2_dev, ym2_dev = dev(z, (y + 2) % NY, x, c), dev(z, (y + 6) % NY, x, c)
    yp3_dev, ym3_dev = dev(z, (y + 3) % NY, x, c), dev(z, (y + 5) % NY, x, c)
    y4_dev = dev(z, (y + 4) % NY, x, c)
    zp_dev, zm_dev = dev((z + 1) % NZ, y, x, c), dev((z + 11) % NZ, y, x, c)

    barrier = pltpu.get_barrier_semaphore()
    near = [
        y4_dev, yp3_dev, ym3_dev, yp2_dev, ym2_dev, x2_dev, xp_dev, xm_dev, yp_dev, ym_dev, zp_dev, zm_dev, core_dev,
    ]
    for target in near:
        pl.semaphore_signal(barrier, inc=1, device_id=target, device_id_type=MESH)
    pl.semaphore_wait(barrier, len(near))

    def remote(src, dst, ssem, rsem, target):
        return pltpu.make_async_remote_copy(
            src_ref=src, dst_ref=dst, send_sem=ssem, recv_sem=rsem,
            device_id=target, device_id_type=MESH,
        )

    started = []

    def send(src, dst, ssem, rsem, target):
        copy = remote(src, dst, ssem, rsem, target)
        copy.start()
        started.append(copy)
        return copy

    col = pl.ds(pl.multiple_of(c * 256, 256), 256)
    other_col = pl.ds(pl.multiple_of((1 - c) * 256, 256), 256)
    wide = pl.ds(pl.multiple_of(c * 1024, 1024), 1024)
    other_wide = pl.ds(pl.multiple_of((1 - c) * 1024, 1024), 1024)

    ek = send(k_hbm.at[:, other_col], kall.at[s], es.at[0], er.at[0], core_dev)
    lk = pltpu.make_async_copy(k_hbm.at[:, col], kall.at[s], lsem.at[0])
    lk.start()
    w_own = w_hbm.at[:, col]
    send(w_own, wbuf.at[f], wzs.at[0, 0, 0], wzr.at[0, 0, 0], zp_dev)
    send(w_own, wbuf.at[f], wzs.at[1, 0, 0], wzr.at[1, 0, 0], zm_dev)
    wy = [
        None,
        send(w_own, wbuf.at[f], wys.at[1], wyr.at[1], ym_dev),
        send(w_own, wbuf.at[f], wys.at[2], wyr.at[2], yp2_dev),
        send(w_own, wbuf.at[f], wys.at[3], wyr.at[3], yp_dev),
    ]
    lw = pltpu.make_async_copy(w_own, wbuf.at[f], lsem.at[1])
    lw.start()
    eq = send(q_hbm.at[:, other_wide], q2.at[c], es.at[1], er.at[1], core_dev)
    lq = pltpu.make_async_copy(q_hbm.at[:, wide], q2.at[c], lsem.at[2])
    lq.start()
    ed = send(do_hbm.at[:, other_wide], do2.at[c], es.at[2], er.at[2], core_dev)
    ld = pltpu.make_async_copy(do_hbm.at[:, wide], do2.at[c], lsem.at[3])
    ld.start()
    et = send(tok_hbm, tok2.at[c], es.at[3], er.at[3], core_dev)
    lt = pltpu.make_async_copy(tok_hbm, tok2.at[c], lsem.at[4])
    lt.start()

    def unit(row, column, block):
        return 2 * (row * NX + column) + block

    def gather_y(buf, ss, rs):
        out = []
        for block, sem in ((0, 0), (1, 9)):
            own = buf.at[unit(yh, x, block)]
            out.append(send(own, own, ss.at[sem], rs.at[sem], y4_dev))
        return out

    def gather_x(buf, ss, rs):
        out = []
        for block, sem, target in ((0, 1, xp_dev), (1, 2, xm_dev), (1, 12, xp_dev), (0, 13, xm_dev)):
            own = buf.at[unit(yh, x, block)]
            out.append(send(own, own, ss.at[sem], rs.at[sem], target))
        return out

    def gather_x_forward(buf, ss, rs, first):
        first[0].wait_recv()
        a = buf.at[unit(yh, xm, 0)]
        up = send(a, a, ss.at[5], rs.at[5], xp_dev)
        first[1].wait_recv()
        b = buf.at[unit(yh, xp, 1)]
        down = send(b, b, ss.at[6], rs.at[6], xm_dev)
        return [first[2], first[3], up, down]

    def gather_peer(buf, ss, rs, from_y, block):
        from_y[block].wait_recv()
        peer = buf.at[unit(1 - yh, x, block)]
        sems = (3, 4) if block == 0 else (10, 11)
        out = [
            send(peer, peer, ss.at[sems[0]], rs.at[sems[0]], xp_dev),
            send(peer, peer, ss.at[sems[1]], rs.at[sems[1]], xm_dev),
        ]
        return out

    def gather_peer_forward(buf, ss, rs, peer, block):
        if block == 0:
            peer[0].wait_recv()
            a = buf.at[unit(1 - yh, xm, 0)]
            return [peer[1], send(a, a, ss.at[7], rs.at[7], xp_dev)]
        peer[1].wait_recv()
        b = buf.at[unit(1 - yh, xp, 1)]
        return [peer[0], send(b, b, ss.at[8], rs.at[8], xm_dev)]

    def ring_plus(t, i):
        at = ((z + NZ - (t - 1)) % NZ) * NYL + (yl + i) % NYL
        return remote(wbuf.at[at], wbuf.at[at], wzs.at[0, t - 1, i], wzr.at[0, t - 1, i], zp_dev)

    def ring_minus(t, i):
        at = ((z + t - 1) % NZ) * NYL + (yl + i) % NYL
        return remote(wbuf.at[at], wbuf.at[at], wzs.at[1, t - 1, i], wzr.at[1, t - 1, i], zm_dev)

    def ring_step(t):
        for i in (0, 1, 3, 2):
            ring_plus(t - 1, i).wait_recv()
            copy = ring_plus(t, i)
            copy.start()
            started.append(copy)
            ring_minus(t - 1, i).wait_recv()
            if t <= 5:
                copy = ring_minus(t, i)
                copy.start()
                started.append(copy)

    lk.wait()
    ek.wait_recv()
    k_y = gather_y(kall, ks, kr)
    k_x = gather_x(kall, ks, kr)

    places = [plan_ref[0, 2 * chip + b] for b in range(2)]
    key_at = []
    row_i = lax.broadcasted_iota(jnp.int32, (BLOCK, BLOCK), 0)
    col_i = lax.broadcasted_iota(jnp.int32, (BLOCK, BLOCK), 1)
    for b in range(2):
        rows = docs_ref[pl.ds(places[b], 1), :].astype(F32)
        ats = []
        for j in range(5):
            place = places[b] - j
            at = jnp.int32(0)
            for t in range(16):
                at = jnp.where(plan_ref[0, t] == place, t, at)
            ats.append(at)
            keys = docs_ref[pl.ds(jnp.maximum(place, 0), 1), :].astype(F32)
            keys = jnp.where(place >= 0, keys, jnp.float32(-1.0))
            keys = jnp.broadcast_to(keys, (BLOCK, BLOCK))
            column = jnp.sum(jnp.where(row_i == col_i, keys, 0.0), axis=1, keepdims=True)
            seen = jnp.broadcast_to(column, (BLOCK, BLOCK)) == jnp.broadcast_to(rows, (BLOCK, BLOCK))
            if j == 0:
                seen = seen & (row_i <= col_i)
            bias[b, pl.ds(j * BLOCK, BLOCK), :] = jnp.where(seen, jnp.float32(0.0), jnp.float32(-jnp.inf))
        key_at.append(ats)
    for i in (1, 3, 2):
        wy[i].wait_recv()
        for copy in (ring_plus(1, i), ring_minus(1, i)):
            copy.start()
            started.append(copy)
    k_rest = gather_x_forward(kall, ks, kr, k_x)
    k_peer0 = gather_peer(kall, ks, kr, k_y, 0)
    ring_step(2)
    k_peer1 = gather_peer(kall, ks, kr, k_y, 1)
    k_rest += gather_peer_forward(kall, ks, kr, k_peer0, 0)
    ring_step(3)
    k_rest += gather_peer_forward(kall, ks, kr, k_peer1, 1)
    lq.wait()
    eq.wait_recv()
    ld.wait()
    ed.wait_recv()
    ring_step(4)
    for copy in k_rest:
        copy.wait_recv()

    def weigh(b):
        def group(g):
            lanes = pl.ds(g * HD, HD)
            keys = jnp.concatenate([kall[at, :, lanes] for at in key_at[b]], axis=0)
            total = jnp.zeros((5 * BLOCK, HD), F32)
            for h in range(GROUP):
                head = pl.ds(pl.multiple_of((g * GROUP + h) * HD, HD), HD)
                scores = lax.dot_general(
                    keys, q2[b, :, head], (((1,), (1,)), ((), ())), preferred_element_type=F32
                ) + bias[b]
                peak = jnp.max(scores, axis=0, keepdims=True)
                exponent = jnp.exp2((scores - peak) * F32(HD ** -0.5 * LOG2E))
                inverse = 1.0 / jnp.sum(exponent, axis=0, keepdims=True)
                weights = (exponent * inverse).astype(BF16)
                wts[b, g * GROUP + h] = weights
                total = total + jnp.dot(weights, do2[b, :, head], preferred_element_type=F32)
            for j in range(5):
                slots[b, j, :, lanes] = total[j * BLOCK:(j + 1) * BLOCK]

        return group

    weigh(0)(0)
    ring_step(5)
    weigh(0)(1)
    weigh(1)(0)
    ring_step(6)
    weigh(1)(1)
    for b in range(2):
        slots[b, 5] = jnp.zeros((BLOCK, 256), F32)

    def lay(t, carry):
        place = plan_ref[0, t]
        parts = []
        for b in range(2):
            j = places[b] - place
            j = jnp.where((j >= 0) & (j <= 4), j, 5)
            parts.append(slots[b, j])
        dvs[t // 8, (t // 2) % NX, t % 2] = (parts[0] + parts[1]).astype(BF16)
        return carry

    lax.fori_loop(0, 16, lay, 0)

    sides = (1 - yh, yh)

    def dv_send(src, number, side, target):
        return send(src, dvr.at[number, side], ds_.at[number, side], dr.at[number, side], target)

    far, close, joint = [], [], []
    for side in range(2):
        far.append((
            dv_send(dvs.at[sides[side], x2, 0], 0, side, xp_dev),
            dv_send(dvs.at[sides[side], x2, 1], 1, side, xm_dev),
        ))
        if side == 0:
            close.append((
                dv_send(dvs.at[sides[side], xp, 1], 2, side, xp_dev),
                dv_send(dvs.at[sides[side], xm, 0], 3, side, xm_dev),
            ))
    lt.wait()
    et.wait_recv()
    lw.wait()
    for i in range(NYL):
        ring_plus(6, i).wait_recv()
    weight = wbuf[...].reshape(48 * 48, 256)
    for b in range(2):
        vall[2 * chip + b] = jnp.dot(tok2[b], weight, preferred_element_type=F32).astype(BF16)
    v_y = gather_y(vall, vs, vr)

    for side in range(2):
        ends = []
        for way in range(2):
            far[side][way].wait_recv()
            mine = dvs[sides[side], xp, 0] if way == 0 else dvs[sides[side], xm, 1]
            dvt[way, side] = (mine.astype(F32) + dvr[way, side].astype(F32)).astype(BF16)
            ends.append(dv_send(dvt.at[way, side], 4 + way, side, xp_dev if way == 0 else xm_dev))
        joint.append(ends)
        if side == 0:
            close.append((
                dv_send(dvs.at[sides[1], xp, 1], 2, 1, xp_dev),
                dv_send(dvs.at[sides[1], xm, 0], 3, 1, xm_dev),
            ))

    def chip_total(side, b):
        for copy in (close[side][1 - b], joint[side][b]):
            copy.wait_recv()
        one, two = (3, 4) if b == 0 else (2, 5)
        return dvs[sides[side], x, b].astype(F32) + dvr[one, side].astype(F32) + dvr[two, side].astype(F32)

    to_y = []
    for b in range(2):
        vgp[0, b] = chip_total(0, b).astype(BF16)
        to_y.append(send(vgp.at[0, b], vgp.at[1, b], dys.at[b], dyr.at[b], y4_dev))
    v_x = gather_x(vall, vs, vr)
    held_total = [chip_total(1, b) for b in range(2)]
    v_rest = gather_x_forward(vall, vs, vr, v_x)
    value_grad = []
    for b in range(2):
        to_y[b].wait_recv()
        value_grad.append((held_total[b] + vgp[1, b].astype(F32)).astype(BF16))

    for j in range(6):
        lanes = pl.ds(j * 384, 384)
        product = jnp.zeros((384, 256), F32)
        for b in range(2):
            product = product + lax.dot_general(
                tok2[b, :, lanes], value_grad[b], (((0,), (0,)), ((), ())), preferred_element_type=F32
            )
        for a in range(NYL):
            for h in range(2):
                at = (a * 2 + h) * 24
                pair = jnp.concatenate(
                    [product[at:at + 24, 0:HD], product[192 + at:192 + at + 24, 0:HD]], axis=0
                )
                gs[h * NYL + a, pl.ds(j * 48, 48), :] = pair.astype(BF16)
        gb[pl.ds(j * 384, 384), :] = product[:, HD:2 * HD]

    halves = (pl.ds(0, 144), pl.ds(144, 144))
    streams = ((0, 0, 4), (1, 1, 4), (0, 1, 3), (1, 0, 3))
    y_dev = (yp_dev, ym_dev)

    def y_dest(direction, distance):
        return (y + distance) % NY if direction == 0 else (y + NY - distance) % NY

    def y_send(stream, hop):
        direction, half, hops = streams[stream]
        at = y_dest(direction, hops - hop)
        return send(
            gs.at[at, halves[half]], gr.at[stream, hop], gys.at[stream, hop], gyr.at[stream, hop], y_dev[direction]
        )

    def y_hop(hop):
        for stream in range(4):
            direction, half, hops = streams[stream]
            if hop >= hops:
                continue
            flying[stream].wait_recv()
            at = y_dest(direction, hops - hop)
            gs[at, halves[half], :] = (
                gs[at, halves[half], :].astype(F32) + gr[stream, hop - 1].astype(F32)
            ).astype(BF16)
            flying[stream] = y_send(stream, hop)

    flying = [y_send(stream, 0) for stream in range(4)]

    for j in range(NZ):
        for a in range(NYL):
            for h in range(2):
                for k in range(NX):
                    to = (h * NYL + a) * 72 + j * 6
                    xb[k, pl.ds(to, 6), :] = gb[pl.ds(j * 192 + (a * 2 + h) * 24 + k * 6, 6), :]
    for k in range(NX):
        xbs[k] = xb[k].astype(BF16)
    sides_b = (pl.ds(0, 288), pl.ds(288, 288))

    def b_send(src, number, target):
        return send(src, xbr.at[number], bs.at[number], br.at[number], target)

    b_far = [
        b_send(xbs.at[x2, sides_b[0]], 0, xp_dev),
        b_send(xbs.at[x2, sides_b[1]], 1, xm_dev),
    ]
    b_close = [
        b_send(xbs.at[xp, sides_b[1]], 2, xp_dev),
        b_send(xbs.at[xm, sides_b[0]], 3, xm_dev),
    ]
    b_far[0].wait_recv()
    xbt[0] = (xb[xp, sides_b[0], :] + xbr[0].astype(F32)).astype(BF16)
    b_joint = [b_send(xbt.at[0], 4, xp_dev)]
    b_far[1].wait_recv()
    xbt[1] = (xb[xm, sides_b[1], :] + xbr[1].astype(F32)).astype(BF16)
    b_joint.append(b_send(xbt.at[1], 5, xm_dev))
    y_hop(1)
    for copy in (b_close[1], b_joint[0]):
        copy.wait_recv()
    yb[sides_b[0], :] = xb[x, sides_b[0], :] + xbr[3].astype(F32) + xbr[4].astype(F32)
    for copy in (b_close[0], b_joint[1]):
        copy.wait_recv()
    yb[sides_b[1], :] = xb[x, sides_b[1], :] + xbr[2].astype(F32) + xbr[5].astype(F32)
    for k in range(NY):
        ybs[k] = yb[pl.ds(k * 72, 72), :].astype(BF16)
    b_y = []
    for d in (4, 3, 5, 2, 6, 1, 7):
        there = (y + d) % NY
        b_y.append(send(ybs.at[there], ybr.at[d], bys.at[d], byr.at[d], dev(z, there, x, c)))
    y_hop(2)
    v_peer0 = gather_peer(vall, vs, vr, v_y, 0)
    v_peer1 = gather_peer(vall, vs, vr, v_y, 1)
    y_hop(3)
    for stream in range(4):
        flying[stream].wait_recv()
    for half in range(2):
        ysum[halves[half], :] = (
            gs[y, halves[half], :].astype(F32)
            + gr[0 if half == 0 else 2, 3 if half == 0 else 2].astype(F32)
            + gr[3 if half == 0 else 1, 2 if half == 0 else 3].astype(F32)
        )

    for k in range(NX):
        for j in range(NZ):
            xf[k, pl.ds(j * 6, 6), :] = ysum[pl.ds(j * 24 + k * 6, 6), :]
    for k in range(NX):
        xs[k] = xf[k].astype(BF16)
    x_copies = [
        send(xs.at[x2], xr.at[2], xss.at[2], xrs.at[2], x2_dev),
        send(xs.at[xp], xr.at[0], xss.at[0], xrs.at[0], xp_dev),
        send(xs.at[xm], xr.at[1], xss.at[1], xrs.at[1], xm_dev),
    ]
    v_rest += gather_peer_forward(vall, vs, vr, v_peer0, 0)
    v_rest += gather_peer_forward(vall, vs, vr, v_peer1, 1)
    for copy in b_y:
        copy.wait_recv()
    b_total = yb[pl.ds(pl.multiple_of(y * 72, 8), 72), :]
    for d in range(1, NY):
        b_total = b_total + ybr[d].astype(F32)
    bsum[...] = b_total
    for copy in x_copies:
        copy.wait_recv()
    xsum[...] = xf[x] + xr[0].astype(F32) + xr[1].astype(F32) + xr[2].astype(F32)

    zs[...] = jnp.zeros((NZ, 2, 8, HD), F32)
    for j in range(NZ):
        for core in range(2):
            at = pl.ds(j * 6 + core * 3, 3)
            zs[j, core, 0:3, :] = xsum[at, :]
            zs[j, core, 3:6, :] = bsum[at, :]

    z_copies = []
    for d in (6, 5, 7, 4, 8, 3, 9, 2, 10, 1, 11, 0):
        there = (z + d) % NZ
        if d > 0:
            z_copies.append(
                send(zs.at[there, c], zr.at[0, d], zss.at[0, d], zrs.at[0, d], dev(there, y, x, c))
            )
        z_copies.append(
            send(zs.at[there, 1 - c], zr.at[1, d], zss.at[1, d], zrs.at[1, d], dev(there, y, x, 1 - c))
        )

    for copy in v_rest:
        copy.wait_recv()

    def attend(b):
        def group(g, carry):
            lanes = pl.ds(pl.multiple_of(g * HD, HD), HD)
            held = jnp.concatenate([vall[at, :, lanes] for at in key_at[b]], axis=0)
            for h in range(GROUP):
                head = pl.ds(pl.multiple_of((g * GROUP + h) * HD, HD), HD)
                flipped = lax.dot_general(
                    held, wts[b, g * GROUP + h], (((0,), (0,)), ((), ())), preferred_element_type=F32
                )
                att2[b, :, head] = flipped.T.astype(BF16)
            return carry

        lax.fori_loop(0, 2, group, 0)

    attend(0)
    attend(1)
    la = pltpu.make_async_copy(att2.at[c], att_out.at[:, wide], lsem.at[5])
    la.start()
    ea = send(att2.at[1 - c], att_out.at[:, wide], es.at[4], er.at[4], core_dev)
    for copy in z_copies:
        copy.wait_recv()
    mine, theirs = zs[z, c], zr[1, 0]
    for d in range(1, NZ):
        mine = mine + zr[0, d]
        theirs = theirs + zr[1, d]
    low, high = jnp.where(c == 0, mine, theirs), jnp.where(c == 0, theirs, mine)
    wg_out[:, 0:128] = low[0:3]
    wg_out[:, 128:256] = low[3:6]
    wg_out[:, 256:384] = high[0:3]
    wg_out[:, 384:512] = high[3:6]
    la.wait()
    ea.wait_recv()
    for copy in started:
        copy.wait_send()


def shards(tokens, queries, key_rows, out_grad, value_weight, documents, block_plan):
    anywhere = pl.BlockSpec(memory_space=pl.ANY)
    in_vmem = pl.BlockSpec(memory_space=pltpu.VMEM)
    dma = pltpu.SemaphoreType.DMA
    vmem = pltpu.VMEM
    attended, weight_grad = pl.pallas_call(
        body,
        out_shape=(
            jax.ShapeDtypeStruct((BLOCK, 2048), BF16),
            jax.ShapeDtypeStruct((3, 512), F32),
        ),
        in_specs=[anywhere] * 5 + [in_vmem, pl.BlockSpec(memory_space=pltpu.SMEM)],
        out_specs=(anywhere, in_vmem),
        scratch_shapes=[
            vmem((2, BLOCK, 2304), BF16),
            vmem((2, BLOCK, 1024), BF16),
            vmem((2, BLOCK, 1024), BF16),
            vmem((16, BLOCK, 256), BF16),
            vmem((16, BLOCK, 256), BF16),
            vmem((48, 48, 256), BF16),
            vmem((2, 5 * BLOCK, BLOCK), F32),
            vmem((2, 8, 5 * BLOCK, BLOCK), BF16),
            vmem((2, 6, BLOCK, 256), F32),
            vmem((2, NX, 2, BLOCK, 256), BF16),
            vmem((6, 2, BLOCK, 256), BF16),
            vmem((2, 2, BLOCK, 256), BF16),
            vmem((2, 2, BLOCK, 256), BF16),
            vmem((2, BLOCK, 1024), BF16),
            vmem((NY, 288, HD), BF16),
            vmem((4, 4, 144, HD), BF16),
            vmem((288, HD), F32),
            vmem((NX, 72, HD), F32),
            vmem((NX, 72, HD), BF16),
            vmem((3, 72, HD), BF16),
            vmem((72, HD), F32),
            vmem((2304, HD), F32),
            vmem((NX, 576, HD), F32),
            vmem((NX, 576, HD), BF16),
            vmem((6, 288, HD), BF16),
            vmem((2, 288, HD), BF16),
            vmem((576, HD), F32),
            vmem((NY, 72, HD), BF16),
            vmem((NY, 72, HD), BF16),
            vmem((72, HD), F32),
            vmem((NZ, 2, 8, HD), F32),
            vmem((2, NZ, 8, HD), F32),
            dma((6,)),
            dma((5,)), dma((5,)),
            dma((4,)), dma((4,)),
            dma((2, 6, 4)), dma((2, 6, 4)),
            dma((14,)), dma((14,)),
            dma((14,)), dma((14,)),
            dma((6, 2)), dma((6, 2)),
            dma((2,)), dma((2,)),
            dma((4, 4)), dma((4, 4)),
            dma((3,)), dma((3,)),
            dma((6,)), dma((6,)),
            dma((NY,)), dma((NY,)),
            dma((2, NZ)), dma((2, NZ)),
        ],
        compiler_params=pltpu.CompilerParams(
            collective_id=0, has_side_effects=True, vmem_limit_bytes=60 * 1024 * 1024
        ),
        name="value_path",
    )(
        tokens[0], queries[0], key_rows[0], out_grad[0], value_weight,
        documents.reshape(16, BLOCK), block_plan,
    )
    return attended[None], weight_grad


def solution(mesh):
    in_specs = (
        P("fsdp", "seq", None),
        P("fsdp", "seq", None),
        P("fsdp", "seq", None),
        P("fsdp", "seq", None),
        P("fsdp", None),
        P("fsdp", None),
        P("fsdp", None),
    )
    out_specs = (P("fsdp", "seq", None), P(("fsdp", "seq"), None))
    return jax.shard_map(shards, mesh=mesh, in_specs=in_specs, out_specs=out_specs, check_vma=False)
```

```python
import jax
import jax.numpy as jnp
from jax import lax
from jax.experimental import pallas as pl
from jax.experimental.pallas import tpu as pltpu
from jax.sharding import PartitionSpec as P

BLOCK = 128
HD = 128
GROUP = 4
NX, NY, NZ, NYL = 4, 8, 12, 4
LOG2E = 1.4426950408889634
BF16 = jnp.bfloat16
F32 = jnp.float32
MESH = pl.DeviceIdType.MESH


def body(
    tok_hbm, q_hbm, k_hbm, do_hbm, w_hbm, docs_ref, plan_ref,
    att_out, wg_out,
    tok2, q2, do2, kall0, kall1, vall, wbuf, bias, wts, slots, dvs, dvr, dvt, vgp, att2,
    gb, xb, xbs, xbr, xbt, yb, ybs, ybr, bsum, zs, zr,
    lsem, es, er, wys, wyr, wzs, wzr, ks, kr, vs, vr, ds_, dr, dys, dyr, bs, br, bys, byr, zss, zrs,
):
    f = lax.axis_index("fsdp")
    s = lax.axis_index("seq")
    z, yl = f // NYL, f % NYL
    yh, x, c = s // 8, (s // 2) % NX, s % 2
    y = yh * NYL + yl
    chip = s // 2

    def dev(z_, y_, x_, c_):
        return (z_ * NYL + y_ % NYL, (y_ // NYL) * 8 + x_ * 2 + c_)

    xp, xm, x2 = (x + 1) % NX, (x + 3) % NX, (x + 2) % NX
    core_dev = dev(z, y, x, 1 - c)
    xp_dev, xm_dev, x2_dev = dev(z, y, xp, c), dev(z, y, xm, c), dev(z, y, x2, c)
    yp_dev, ym_dev = dev(z, (y + 1) % NY, x, c), dev(z, (y + 7) % NY, x, c)
    yp2_dev, ym2_dev = dev(z, (y + 2) % NY, x, c), dev(z, (y + 6) % NY, x, c)
    yp3_dev, ym3_dev = dev(z, (y + 3) % NY, x, c), dev(z, (y + 5) % NY, x, c)
    y4_dev = dev(z, (y + 4) % NY, x, c)
    crossed = [dev(z, (y + 4) % NY, x, 1 - c), dev(z, y, xp, 1 - c), dev(z, y, xm, 1 - c)]
    zp_dev, zm_dev = dev((z + 1) % NZ, y, x, c), dev((z + 11) % NZ, y, x, c)

    barrier = pltpu.get_barrier_semaphore()
    near = [
        y4_dev, yp3_dev, ym3_dev, yp2_dev, ym2_dev, x2_dev, xp_dev, xm_dev, yp_dev, ym_dev, zp_dev, zm_dev, core_dev,
    ] + crossed
    for target in near:
        pl.semaphore_signal(barrier, inc=1, device_id=target, device_id_type=MESH)
    pl.semaphore_wait(barrier, len(near))

    def remote(src, dst, ssem, rsem, target):
        return pltpu.make_async_remote_copy(
            src_ref=src, dst_ref=dst, send_sem=ssem, recv_sem=rsem,
            device_id=target, device_id_type=MESH,
        )

    started = []

    def send(src, dst, ssem, rsem, target):
        copy = remote(src, dst, ssem, rsem, target)
        copy.start()
        started.append(copy)
        return copy

    col = pl.ds(pl.multiple_of(c * 256, 256), 256)
    other_col = pl.ds(pl.multiple_of((1 - c) * 256, 256), 256)
    wide = pl.ds(pl.multiple_of(c * 1024, 1024), 1024)
    other_wide = pl.ds(pl.multiple_of((1 - c) * 1024, 1024), 1024)

    w_own = w_hbm.at[:, col]
    send(w_own, wbuf.at[f], wzs.at[0, 0, 0], wzr.at[0, 0, 0], zp_dev)
    send(w_own, wbuf.at[f], wzs.at[1, 0, 0], wzr.at[1, 0, 0], zm_dev)
    wy = [
        None,
        send(w_own, wbuf.at[f], wys.at[1], wyr.at[1], ym_dev),
        send(w_own, wbuf.at[f], wys.at[2], wyr.at[2], yp2_dev),
        send(w_own, wbuf.at[f], wys.at[3], wyr.at[3], yp_dev),
    ]
    lw = pltpu.make_async_copy(w_own, wbuf.at[f], lsem.at[1])
    lw.start()
    first_x, last_x = jnp.where(c == 0, xp, xm), jnp.where(c == 0, xm, xp)
    kall = (kall0, kall1)
    key_local, key_core = [], []
    for g in range(2):
        k_own = k_hbm.at[:, pl.ds(pl.multiple_of(c * 256 + g * HD, HD), HD)]
        k_other = k_hbm.at[:, pl.ds(pl.multiple_of((1 - c) * 256 + g * HD, HD), HD)]

        def key_out(kind, targets):
            send(k_own, kall[g].at[s], ks.at[g, kind, 0], kr.at[g, kind, c], targets[0])
            send(k_other, kall[g].at[s], ks.at[g, kind, 1], kr.at[g, kind, c], targets[1])

        key_out(0, (y4_dev, crossed[0]))
        key_core.append(send(k_other, kall[g].at[s], es.at[5 + g], er.at[5 + g], core_dev))
        copy = pltpu.make_async_copy(k_own, kall[g].at[s], lsem.at[6 + g])
        copy.start()
        key_local.append(copy)
        key_out(1 + c, (dev(z, y, first_x, c), dev(z, y, first_x, 1 - c)))
        key_out(2 - c, (dev(z, y, last_x, c), dev(z, y, last_x, 1 - c)))

    def unit(row, column, block):
        return 2 * (row * NX + column) + block

    def arrived(buf, ss, rs, kind, block):
        return remote(buf.at[0], buf.at[0], ss.at[kind, block], rs.at[kind, block], core_dev)

    def gather_y(buf, ss, rs):
        for block in range(2):
            own = buf.at[unit(yh, x, block)]
            send(own, own, ss.at[0, block], rs.at[0, block], y4_dev)

    def gather_x(buf, ss, rs):
        for block, kind, target in ((0, 1, xp_dev), (1, 2, xm_dev), (1, 1, xp_dev), (0, 2, xm_dev)):
            own = buf.at[unit(yh, x, block)]
            send(own, own, ss.at[kind, block], rs.at[kind, block], target)

    def pass_on(buf, ss, rs, row, kinds, number):
        arrived(buf, ss, rs, kinds[0], 0).wait_recv()
        a = buf.at[unit(row, xm, 0)]
        send(a, a, ss.at[number, 0], rs.at[number, 0], xp_dev)
        arrived(buf, ss, rs, kinds[1], 1).wait_recv()
        b = buf.at[unit(row, xp, 1)]
        send(b, b, ss.at[number, 1], rs.at[number, 1], xm_dev)

    def gather_x_forward(buf, ss, rs):
        pass_on(buf, ss, rs, yh, (1, 2), 5)

    def gather_peer(buf, ss, rs, block):
        arrived(buf, ss, rs, 0, block).wait_recv()
        peer = buf.at[unit(1 - yh, x, block)]
        for kind, target in ((3, xp_dev), (4, xm_dev)) if block == 0 else ((4, xm_dev), (3, xp_dev)):
            send(peer, peer, ss.at[kind, block], rs.at[kind, block], target)

    def gather_peer_forward(buf, ss, rs):
        pass_on(buf, ss, rs, 1 - yh, (3, 4), 6)

    def gather_done(buf, ss, rs):
        for kind, block in ((1, 1), (2, 0), (5, 0), (5, 1), (3, 1), (4, 0), (6, 0), (6, 1)):
            arrived(buf, ss, rs, kind, block).wait_recv()

    def ring_plus(t, i):
        at = ((z + NZ - (t - 1)) % NZ) * NYL + (yl + i) % NYL
        return remote(wbuf.at[at], wbuf.at[at], wzs.at[0, t - 1, i], wzr.at[0, t - 1, i], zp_dev)

    def ring_minus(t, i):
        at = ((z + t - 1) % NZ) * NYL + (yl + i) % NYL
        return remote(wbuf.at[at], wbuf.at[at], wzs.at[1, t - 1, i], wzr.at[1, t - 1, i], zm_dev)

    def ring_step(t):
        for i in (0, 1, 3, 2):
            ring_plus(t - 1, i).wait_recv()
            copy = ring_plus(t, i)
            copy.start()
            started.append(copy)
            ring_minus(t - 1, i).wait_recv()
            if t <= 5:
                copy = ring_minus(t, i)
                copy.start()
                started.append(copy)

    places = [plan_ref[0, 2 * chip + b] for b in range(2)]
    key_at = []
    row_i = lax.broadcasted_iota(jnp.int32, (BLOCK, BLOCK), 0)
    col_i = lax.broadcasted_iota(jnp.int32, (BLOCK, BLOCK), 1)
    for b in range(2):
        rows = docs_ref[pl.ds(places[b], 1), :].astype(F32)
        ats = []
        for j in range(5):
            place = places[b] - j
            at = jnp.int32(0)
            for t in range(16):
                at = jnp.where(plan_ref[0, t] == place, t, at)
            ats.append(at)
            keys = docs_ref[pl.ds(jnp.maximum(place, 0), 1), :].astype(F32)
            keys = jnp.where(place >= 0, keys, jnp.float32(-1.0))
            keys = jnp.broadcast_to(keys, (BLOCK, BLOCK))
            column = jnp.sum(jnp.where(row_i == col_i, keys, 0.0), axis=1, keepdims=True)
            seen = jnp.broadcast_to(column, (BLOCK, BLOCK)) == jnp.broadcast_to(rows, (BLOCK, BLOCK))
            if j == 0:
                seen = seen & (row_i <= col_i)
            bias[b, pl.ds(j * BLOCK, BLOCK), :] = jnp.where(seen, jnp.float32(0.0), jnp.float32(-jnp.inf))
        key_at.append(ats)
    keys_of = [(kall[g], ks.at[g], kr.at[g]) for g in range(2)]
    gather_x_forward(*keys_of[0])
    for i in (1, 3, 2):
        wy[i].wait_recv()
        for copy in (ring_plus(1, i), ring_minus(1, i)):
            copy.start()
            started.append(copy)
    eq = send(q_hbm.at[:, other_wide], q2.at[c], es.at[1], er.at[1], core_dev)
    lq = pltpu.make_async_copy(q_hbm.at[:, wide], q2.at[c], lsem.at[2])
    lq.start()
    ed = send(do_hbm.at[:, other_wide], do2.at[c], es.at[2], er.at[2], core_dev)
    ld = pltpu.make_async_copy(do_hbm.at[:, wide], do2.at[c], lsem.at[3])
    ld.start()
    et = send(tok_hbm, tok2.at[c], es.at[3], er.at[3], core_dev)
    lt = pltpu.make_async_copy(tok_hbm, tok2.at[c], lsem.at[4])
    lt.start()

    gather_x_forward(*keys_of[1])
    gather_peer(*keys_of[0], 0)
    gather_peer(*keys_of[0], 1)
    ring_step(2)
    gather_peer_forward(*keys_of[0])
    gather_peer(*keys_of[1], 0)
    gather_peer(*keys_of[1], 1)
    lq.wait()
    eq.wait_recv()
    ld.wait()
    ed.wait_recv()
    key_local[0].wait()
    key_core[0].wait_recv()
    gather_done(*keys_of[0])
    ring_step(3)

    def weigh(b):
        def group(g):
            lanes = pl.ds(g * HD, HD)
            keys = jnp.concatenate([kall[g][at] for at in key_at[b]], axis=0)
            total = jnp.zeros((5 * BLOCK, HD), F32)
            for h in range(GROUP):
                head = pl.ds(pl.multiple_of((g * GROUP + h) * HD, HD), HD)
                scores = lax.dot_general(
                    keys, q2[b, :, head], (((1,), (1,)), ((), ())), preferred_element_type=F32
                ) + bias[b]
                peak = jnp.max(scores, axis=0, keepdims=True)
                exponent = jnp.exp2((scores - peak) * F32(HD ** -0.5 * LOG2E))
                inverse = 1.0 / jnp.sum(exponent, axis=0, keepdims=True)
                weights = (exponent * inverse).astype(BF16)
                wts[b, g * GROUP + h] = weights
                total = total + jnp.dot(weights, do2[b, :, head], preferred_element_type=F32)
            for j in range(5):
                slots[b, j, :, lanes] = total[j * BLOCK:(j + 1) * BLOCK]

        return group

    for b in range(2):
        slots[b, 5] = jnp.zeros((BLOCK, 256), F32)

    def lay(g):
        lanes = pl.ds(g * HD, HD)

        def one(t, carry):
            place = plan_ref[0, t]
            parts = []
            for b in range(2):
                j = places[b] - place
                j = jnp.where((j >= 0) & (j <= 4), j, 5)
                parts.append(slots[b, j, :, lanes])
            dvs[g, t // 8, (t // 2) % NX, t % 2] = (parts[0] + parts[1]).astype(BF16)
            return carry

        lax.fori_loop(0, 16, one, 0)

    sides = (1 - yh, yh)
    far, close, joint, to_y, held_total = {}, {}, {}, {}, {}

    def dv_send(g, src, number, side, target):
        return send(src, dvr.at[g, number, side], ds_.at[g, number, side], dr.at[g, number, side], target)

    def dv_out(g, side):
        row = sides[side]
        far[g, side] = (
            dv_send(g, dvs.at[g, row, x2, 0], 0, side, xp_dev),
            dv_send(g, dvs.at[g, row, x2, 1], 1, side, xm_dev),
        )
        close[g, side] = (
            dv_send(g, dvs.at[g, row, xp, 1], 2, side, xp_dev),
            dv_send(g, dvs.at[g, row, xm, 0], 3, side, xm_dev),
        )

    def dv_join(g, side):
        out = []
        for way in range(2):
            far[g, side][way].wait_recv()
            mine = dvs[g, sides[side], xp, 0] if way == 0 else dvs[g, sides[side], xm, 1]
            dvt[g, way, side] = (mine.astype(F32) + dvr[g, way, side].astype(F32)).astype(BF16)
            out.append(dv_send(g, dvt.at[g, way, side], 4 + way, side, xp_dev if way == 0 else xm_dev))
        joint[g, side] = out

    def chip_total(g, side, b):
        for copy in (close[g, side][1 - b], joint[g, side][b]):
            copy.wait_recv()
        one, two = (3, 4) if b == 0 else (2, 5)
        return (
            dvs[g, sides[side], x, b].astype(F32)
            + dvr[g, one, side].astype(F32)
            + dvr[g, two, side].astype(F32)
        )

    def dv_peer(g):
        to_y[g] = []
        for b in range(2):
            vgp[g, 0, b] = chip_total(g, 0, b).astype(BF16)
            to_y[g].append(send(vgp.at[g, 0, b], vgp.at[g, 1, b], dys.at[g, b], dyr.at[g, b], y4_dev))

    def dv_own(g):
        held_total[g] = [chip_total(g, 1, b) for b in range(2)]

    def dv_final(g):
        out = []
        for b in range(2):
            to_y[g][b].wait_recv()
            out.append((held_total[g][b] + vgp[g, 1, b].astype(F32)).astype(BF16))
        return out

    weigh(0)(0)
    weigh(1)(0)
    lay(0)
    dv_out(0, 0)
    gather_peer_forward(*keys_of[1])
    dv_join(0, 0)
    dv_out(0, 1)
    key_local[1].wait()
    key_core[1].wait_recv()
    gather_done(*keys_of[1])
    ring_step(4)
    weigh(0)(1)
    weigh(1)(1)
    lay(1)
    dv_out(1, 0)
    dv_peer(0)
    dv_join(0, 1)
    dv_join(1, 0)
    dv_out(1, 1)
    ring_step(5)
    dv_own(0)
    dv_peer(1)
    dv_join(1, 1)
    ring_step(6)

    def product_of(part, value_grad):
        for j in range(6):
            lanes = pl.ds(j * 384, 384)
            product = jnp.zeros((384, HD), F32)
            for b in range(2):
                product = product + lax.dot_general(
                    tok2[b, :, lanes], value_grad[b], (((0,), (0,)), ((), ())), preferred_element_type=F32
                )
            gb[part, pl.ds(j * 384, 384), :] = product

    ends = (pl.ds(0, 288), pl.ds(288, 288))

    def regroup(part):
        for j in range(NZ):
            for a in range(NYL):
                for h in range(2):
                    for k in range(NX):
                        to = (h * NYL + a) * 72 + j * 6
                        xb[part, k, pl.ds(to, 6), :] = gb[part, pl.ds(j * 192 + (a * 2 + h) * 24 + k * 6, 6), :]
        for k in range(NX):
            xbs[part, k] = xb[part, k].astype(BF16)

    def g_send(part, src, number, target):
        return send(src, xbr.at[part, number], bs.at[part, number], br.at[part, number], target)

    def g_far(part):
        return [
            g_send(part, xbs.at[part, x2, ends[0]], 0, xp_dev),
            g_send(part, xbs.at[part, x2, ends[1]], 1, xm_dev),
        ]

    def g_close(part):
        return [
            g_send(part, xbs.at[part, xp, ends[1]], 2, xp_dev),
            g_send(part, xbs.at[part, xm, ends[0]], 3, xm_dev),
        ]

    def g_join(part, copies):
        out = []
        for way, at, target in ((0, xp, xp_dev), (1, xm, xm_dev)):
            copies[way].wait_recv()
            xbt[part, way] = (xb[part, at, ends[way], :] + xbr[part, way].astype(F32)).astype(BF16)
            out.append(g_send(part, xbt.at[part, way], 4 + way, target))
        return out

    def g_total(part, close_pair, joint_pair):
        for end, one, two in ((0, 3, 4), (1, 2, 5)):
            close_pair[1 - end].wait_recv()
            joint_pair[end].wait_recv()
            yb[part, ends[end], :] = (
                xb[part, x, ends[end], :] + xbr[part, one].astype(F32) + xbr[part, two].astype(F32)
            )
        for k in range(NY):
            ybs[part, k] = yb[part, pl.ds(k * 72, 72), :].astype(BF16)
        out = []
        for d in (4, 3, 5, 2, 6, 1, 7):
            there = (y + d) % NY
            out.append(
                send(ybs.at[part, there], ybr.at[part, d], bys.at[part, d], byr.at[part, d], dev(z, there, x, c))
            )
        return out

    lt.wait()
    et.wait_recv()
    value_grad = dv_final(0)
    product_of(0, value_grad)
    regroup(0)
    far0 = g_far(0)
    close0 = g_close(0)
    dv_own(1)
    lw.wait()
    for i in range(NYL):
        ring_plus(6, i).wait_recv()
    weight = wbuf[...].reshape(48 * 48, 256)
    for b in range(2):
        vall[2 * chip + b] = jnp.dot(tok2[b], weight, preferred_element_type=F32).astype(BF16)
    gather_y(vall, vs, vr)
    joint0 = g_join(0, far0)
    value_grad = dv_final(1)
    product_of(1, value_grad)
    regroup(1)
    far1 = g_far(1)
    close1 = g_close(1)

    y0 = g_total(0, close0, joint0)
    joint1 = g_join(1, far1)
    gather_x(vall, vs, vr)
    y1 = g_total(1, close1, joint1)
    gather_peer(vall, vs, vr, 0)
    gather_peer(vall, vs, vr, 1)
    gather_x_forward(vall, vs, vr)
    gather_peer_forward(vall, vs, vr)
    for part, copies in ((0, y0), (1, y1)):
        for copy in copies:
            copy.wait_recv()
        total = yb[part, pl.ds(pl.multiple_of(y * 72, 8), 72), :]
        for d in range(1, NY):
            total = total + ybr[part, d].astype(F32)
        bsum[part] = total

    zs[...] = jnp.zeros((NZ, 2, 8, HD), F32)
    for j in range(NZ):
        for core in range(2):
            at = pl.ds(j * 6 + core * 3, 3)
            zs[j, core, 0:3, :] = bsum[0, at, :]
            zs[j, core, 3:6, :] = bsum[1, at, :]

    z_copies = []
    for d in (6, 5, 7, 4, 8, 3, 9, 2, 10, 1, 11, 0):
        there = (z + d) % NZ
        if d > 0:
            z_copies.append(
                send(zs.at[there, c], zr.at[0, d], zss.at[0, d], zrs.at[0, d], dev(there, y, x, c))
            )
        z_copies.append(
            send(zs.at[there, 1 - c], zr.at[1, d], zss.at[1, d], zrs.at[1, d], dev(there, y, x, 1 - c))
        )

    gather_done(vall, vs, vr)

    def attend(b):
        def group(g, carry):
            lanes = pl.ds(pl.multiple_of(g * HD, HD), HD)
            held = jnp.concatenate([vall[at, :, lanes] for at in key_at[b]], axis=0)
            for h in range(GROUP):
                head = pl.ds(pl.multiple_of((g * GROUP + h) * HD, HD), HD)
                flipped = lax.dot_general(
                    held, wts[b, g * GROUP + h], (((0,), (0,)), ((), ())), preferred_element_type=F32
                )
                att2[b, :, head] = flipped.T.astype(BF16)
            return carry

        lax.fori_loop(0, 2, group, 0)

    attend(0)
    attend(1)
    la = pltpu.make_async_copy(att2.at[c], att_out.at[:, wide], lsem.at[5])
    la.start()
    ea = send(att2.at[1 - c], att_out.at[:, wide], es.at[4], er.at[4], core_dev)
    for copy in z_copies:
        copy.wait_recv()
    mine, theirs = zs[z, c], zr[1, 0]
    for d in range(1, NZ):
        mine = mine + zr[0, d]
        theirs = theirs + zr[1, d]
    low, high = jnp.where(c == 0, mine, theirs), jnp.where(c == 0, theirs, mine)
    wg_out[:, 0:128] = low[0:3]
    wg_out[:, 128:256] = low[3:6]
    wg_out[:, 256:384] = high[0:3]
    wg_out[:, 384:512] = high[3:6]
    la.wait()
    ea.wait_recv()
    for copy in started:
        copy.wait_send()


def shards(tokens, queries, key_rows, out_grad, value_weight, documents, block_plan):
    anywhere = pl.BlockSpec(memory_space=pl.ANY)
    in_vmem = pl.BlockSpec(memory_space=pltpu.VMEM)
    dma = pltpu.SemaphoreType.DMA
    vmem = pltpu.VMEM
    attended, weight_grad = pl.pallas_call(
        body,
        out_shape=(
            jax.ShapeDtypeStruct((BLOCK, 2048), BF16),
            jax.ShapeDtypeStruct((3, 512), F32),
        ),
        in_specs=[anywhere] * 5 + [in_vmem, pl.BlockSpec(memory_space=pltpu.SMEM)],
        out_specs=(anywhere, in_vmem),
        scratch_shapes=[
            vmem((2, BLOCK, 2304), BF16),
            vmem((2, BLOCK, 1024), BF16),
            vmem((2, BLOCK, 1024), BF16),
            vmem((16, BLOCK, HD), BF16),
            vmem((16, BLOCK, HD), BF16),
            vmem((16, BLOCK, 256), BF16),
            vmem((48, 48, 256), BF16),
            vmem((2, 5 * BLOCK, BLOCK), F32),
            vmem((2, 8, 5 * BLOCK, BLOCK), BF16),
            vmem((2, 6, BLOCK, 256), F32),
            vmem((2, 2, NX, 2, BLOCK, HD), BF16),
            vmem((2, 6, 2, BLOCK, HD), BF16),
            vmem((2, 2, 2, BLOCK, HD), BF16),
            vmem((2, 2, 2, BLOCK, HD), BF16),
            vmem((2, BLOCK, 1024), BF16),
            vmem((2, 2304, HD), F32),
            vmem((2, NX, 576, HD), F32),
            vmem((2, NX, 576, HD), BF16),
            vmem((2, 6, 288, HD), BF16),
            vmem((2, 2, 288, HD), BF16),
            vmem((2, 576, HD), F32),
            vmem((2, NY, 72, HD), BF16),
            vmem((2, NY, 72, HD), BF16),
            vmem((2, 72, HD), F32),
            vmem((NZ, 2, 8, HD), F32),
            vmem((2, NZ, 8, HD), F32),
            dma((8,)),
            dma((7,)), dma((7,)),
            dma((4,)), dma((4,)),
            dma((2, 6, 4)), dma((2, 6, 4)),
            dma((2, 7, 2)), dma((2, 7, 2)),
            dma((7, 2)), dma((7, 2)),
            dma((2, 6, 2)), dma((2, 6, 2)),
            dma((2, 2)), dma((2, 2)),
            dma((2, 6)), dma((2, 6)),
            dma((2, NY)), dma((2, NY)),
            dma((2, NZ)), dma((2, NZ)),
        ],
        compiler_params=pltpu.CompilerParams(
            collective_id=0, has_side_effects=True, vmem_limit_bytes=60 * 1024 * 1024
        ),
        name="value_path",
    )(
        tokens[0], queries[0], key_rows[0], out_grad[0], value_weight,
        documents.reshape(16, BLOCK), block_plan,
    )
    return attended[None], weight_grad


def solution(mesh):
    in_specs = (
        P("fsdp", "seq", None),
        P("fsdp", "seq", None),
        P("fsdp", "seq", None),
        P("fsdp", "seq", None),
        P("fsdp", None),
        P("fsdp", None),
        P("fsdp", None),
    )
    out_specs = (P("fsdp", "seq", None), P(("fsdp", "seq"), None))
    return jax.shard_map(shards, mesh=mesh, in_specs=in_specs, out_specs=out_specs, check_vma=False)
```

```python
import jax
import jax.numpy as jnp
from jax import lax
from jax.experimental import pallas as pl
from jax.experimental.pallas import tpu as pltpu
from jax.sharding import PartitionSpec as P

BLOCK = 128
HD = 128
GROUP = 4
NX, NY, NZ, NYL = 4, 8, 12, 4
LOG2E = 1.4426950408889634
BF16 = jnp.bfloat16
F32 = jnp.float32
MESH = pl.DeviceIdType.MESH


def body(
    tok_hbm, q_hbm, k_hbm, do_hbm, w_hbm, docs_ref, plan_ref,
    att_out, wg_out,
    tok2, q2, do2, kall0, kall1, vall, wbuf, bias, wts, slots, dvs, dvr, dvt, vgp, att2,
    gb, xb, xbs, xbr, xbt, yb, ybs, ybr, bsum, zs, zr,
    lsem, es, er, wys, wyr, wzs, wzr, ks, kr, vs, vr, ds_, dr, dys, dyr, bs, br, bys, byr, zss, zrs,
):
    f = lax.axis_index("fsdp")
    s = lax.axis_index("seq")
    z, yl = f // NYL, f % NYL
    yh, x, c = s // 8, (s // 2) % NX, s % 2
    y = yh * NYL + yl
    chip = s // 2

    def dev(z_, y_, x_, c_):
        return (z_ * NYL + y_ % NYL, (y_ // NYL) * 8 + x_ * 2 + c_)

    xp, xm, x2 = (x + 1) % NX, (x + 3) % NX, (x + 2) % NX
    core_dev = dev(z, y, x, 1 - c)
    xp_dev, xm_dev, x2_dev = dev(z, y, xp, c), dev(z, y, xm, c), dev(z, y, x2, c)
    yp_dev, ym_dev = dev(z, (y + 1) % NY, x, c), dev(z, (y + 7) % NY, x, c)
    yp2_dev, ym2_dev = dev(z, (y + 2) % NY, x, c), dev(z, (y + 6) % NY, x, c)
    yp3_dev, ym3_dev = dev(z, (y + 3) % NY, x, c), dev(z, (y + 5) % NY, x, c)
    y4_dev = dev(z, (y + 4) % NY, x, c)
    crossed = [dev(z, (y + 4) % NY, x, 1 - c), dev(z, y, xp, 1 - c), dev(z, y, xm, 1 - c)]
    zp_dev, zm_dev = dev((z + 1) % NZ, y, x, c), dev((z + 11) % NZ, y, x, c)

    barrier = pltpu.get_barrier_semaphore()
    near = [
        y4_dev, yp3_dev, ym3_dev, yp2_dev, ym2_dev, x2_dev, xp_dev, xm_dev, yp_dev, ym_dev, zp_dev, zm_dev, core_dev,
    ] + crossed
    for target in near:
        pl.semaphore_signal(barrier, inc=1, device_id=target, device_id_type=MESH)
    pl.semaphore_wait(barrier, len(near))

    def remote(src, dst, ssem, rsem, target):
        return pltpu.make_async_remote_copy(
            src_ref=src, dst_ref=dst, send_sem=ssem, recv_sem=rsem,
            device_id=target, device_id_type=MESH,
        )

    started = []

    def send(src, dst, ssem, rsem, target):
        copy = remote(src, dst, ssem, rsem, target)
        copy.start()
        started.append(copy)
        return copy

    col = pl.ds(pl.multiple_of(c * 256, 256), 256)
    other_col = pl.ds(pl.multiple_of((1 - c) * 256, 256), 256)
    wide = pl.ds(pl.multiple_of(c * 1024, 1024), 1024)
    other_wide = pl.ds(pl.multiple_of((1 - c) * 1024, 1024), 1024)

    w_own = w_hbm.at[:, col]
    send(w_own, wbuf.at[f], wzs.at[0, 0, 0], wzr.at[0, 0, 0], zp_dev)
    send(w_own, wbuf.at[f], wzs.at[1, 0, 0], wzr.at[1, 0, 0], zm_dev)
    wy = [
        None,
        send(w_own, wbuf.at[f], wys.at[1], wyr.at[1], ym_dev),
        send(w_own, wbuf.at[f], wys.at[2], wyr.at[2], yp2_dev),
        send(w_own, wbuf.at[f], wys.at[3], wyr.at[3], yp_dev),
    ]
    lw = pltpu.make_async_copy(w_own, wbuf.at[f], lsem.at[1])
    lw.start()
    first_x, last_x = jnp.where(c == 0, xp, xm), jnp.where(c == 0, xm, xp)
    kall = (kall0, kall1)
    key_local, key_core = [], []
    for g in range(2):
        k_own = k_hbm.at[:, pl.ds(pl.multiple_of(c * 256 + g * HD, HD), HD)]
        k_other = k_hbm.at[:, pl.ds(pl.multiple_of((1 - c) * 256 + g * HD, HD), HD)]

        def key_out(kind, targets):
            send(k_own, kall[g].at[s], ks.at[g, kind, 0], kr.at[g, kind, c], targets[0])
            send(k_other, kall[g].at[s], ks.at[g, kind, 1], kr.at[g, kind, c], targets[1])

        key_out(0, (y4_dev, crossed[0]))
        key_core.append(send(k_other, kall[g].at[s], es.at[5 + g], er.at[5 + g], core_dev))
        copy = pltpu.make_async_copy(k_own, kall[g].at[s], lsem.at[6 + g])
        copy.start()
        key_local.append(copy)
        key_out(1 + c, (dev(z, y, first_x, c), dev(z, y, first_x, 1 - c)))
        key_out(2 - c, (dev(z, y, last_x, c), dev(z, y, last_x, 1 - c)))

    def unit(row, column, block):
        return 2 * (row * NX + column) + block

    def arrived(buf, ss, rs, kind, block):
        return remote(buf.at[0], buf.at[0], ss.at[kind, block], rs.at[kind, block], core_dev)

    def gather_y(buf, ss, rs):
        for block in range(2):
            own = buf.at[unit(yh, x, block)]
            send(own, own, ss.at[0, block], rs.at[0, block], y4_dev)

    def gather_x(buf, ss, rs):
        for block, kind, target in ((0, 1, xp_dev), (1, 2, xm_dev), (1, 1, xp_dev), (0, 2, xm_dev)):
            own = buf.at[unit(yh, x, block)]
            send(own, own, ss.at[kind, block], rs.at[kind, block], target)

    def pass_on(buf, ss, rs, row, kinds, number):
        arrived(buf, ss, rs, kinds[0], 0).wait_recv()
        a = buf.at[unit(row, xm, 0)]
        send(a, a, ss.at[number, 0], rs.at[number, 0], xp_dev)
        arrived(buf, ss, rs, kinds[1], 1).wait_recv()
        b = buf.at[unit(row, xp, 1)]
        send(b, b, ss.at[number, 1], rs.at[number, 1], xm_dev)

    def gather_x_forward(buf, ss, rs):
        pass_on(buf, ss, rs, yh, (1, 2), 5)

    def gather_peer(buf, ss, rs):
        for block in range(2):
            arrived(buf, ss, rs, 0, block).wait_recv()
        for block, kind, target in ((0, 3, xp_dev), (1, 4, xm_dev), (1, 3, xp_dev), (0, 4, xm_dev)):
            peer = buf.at[unit(1 - yh, x, block)]
            send(peer, peer, ss.at[kind, block], rs.at[kind, block], target)

    def gather_peer_forward(buf, ss, rs):
        pass_on(buf, ss, rs, 1 - yh, (3, 4), 6)

    def gather_done(buf, ss, rs):
        for kind, block in ((1, 1), (2, 0), (5, 0), (5, 1), (3, 1), (4, 0), (6, 0), (6, 1)):
            arrived(buf, ss, rs, kind, block).wait_recv()

    def ring_plus(t, i):
        at = ((z + NZ - (t - 1)) % NZ) * NYL + (yl + i) % NYL
        return remote(wbuf.at[at], wbuf.at[at], wzs.at[0, t - 1, i], wzr.at[0, t - 1, i], zp_dev)

    def ring_minus(t, i):
        at = ((z + t - 1) % NZ) * NYL + (yl + i) % NYL
        return remote(wbuf.at[at], wbuf.at[at], wzs.at[1, t - 1, i], wzr.at[1, t - 1, i], zm_dev)

    def ring_step(t):
        for i in (0, 1, 3, 2):
            ring_plus(t - 1, i).wait_recv()
            copy = ring_plus(t, i)
            copy.start()
            started.append(copy)
            ring_minus(t - 1, i).wait_recv()
            if t <= 5:
                copy = ring_minus(t, i)
                copy.start()
                started.append(copy)

    places = [plan_ref[0, 2 * chip + b] for b in range(2)]
    key_at = []
    row_i = lax.broadcasted_iota(jnp.int32, (BLOCK, BLOCK), 0)
    col_i = lax.broadcasted_iota(jnp.int32, (BLOCK, BLOCK), 1)
    for b in range(2):
        rows = docs_ref[pl.ds(places[b], 1), :].astype(F32)
        ats = []
        for j in range(5):
            place = places[b] - j
            at = jnp.int32(0)
            for t in range(16):
                at = jnp.where(plan_ref[0, t] == place, t, at)
            ats.append(at)
            keys = docs_ref[pl.ds(jnp.maximum(place, 0), 1), :].astype(F32)
            keys = jnp.where(place >= 0, keys, jnp.float32(-1.0))
            keys = jnp.broadcast_to(keys, (BLOCK, BLOCK))
            column = jnp.sum(jnp.where(row_i == col_i, keys, 0.0), axis=1, keepdims=True)
            seen = jnp.broadcast_to(column, (BLOCK, BLOCK)) == jnp.broadcast_to(rows, (BLOCK, BLOCK))
            if j == 0:
                seen = seen & (row_i <= col_i)
            bias[b, pl.ds(j * BLOCK, BLOCK), :] = jnp.where(seen, jnp.float32(0.0), jnp.float32(-jnp.inf))
        key_at.append(ats)
    keys_of = [(kall[g], ks.at[g], kr.at[g]) for g in range(2)]
    gather_x_forward(*keys_of[0])
    for i in (1, 3, 2):
        wy[i].wait_recv()
        for copy in (ring_plus(1, i), ring_minus(1, i)):
            copy.start()
            started.append(copy)
    eq = send(q_hbm.at[:, other_wide], q2.at[c], es.at[1], er.at[1], core_dev)
    lq = pltpu.make_async_copy(q_hbm.at[:, wide], q2.at[c], lsem.at[2])
    lq.start()
    ed = send(do_hbm.at[:, other_wide], do2.at[c], es.at[2], er.at[2], core_dev)
    ld = pltpu.make_async_copy(do_hbm.at[:, wide], do2.at[c], lsem.at[3])
    ld.start()
    et = send(tok_hbm, tok2.at[c], es.at[3], er.at[3], core_dev)
    lt = pltpu.make_async_copy(tok_hbm, tok2.at[c], lsem.at[4])
    lt.start()

    gather_x_forward(*keys_of[1])
    gather_peer(*keys_of[0])
    ring_step(2)
    gather_peer_forward(*keys_of[0])
    gather_peer(*keys_of[1])
    lq.wait()
    eq.wait_recv()
    ld.wait()
    ed.wait_recv()
    key_local[0].wait()
    key_core[0].wait_recv()
    gather_done(*keys_of[0])
    ring_step(3)

    def weigh(b):
        def group(g):
            lanes = pl.ds(g * HD, HD)
            keys = jnp.concatenate([kall[g][at] for at in key_at[b]], axis=0)
            total = jnp.zeros((5 * BLOCK, HD), F32)
            for h in range(GROUP):
                head = pl.ds(pl.multiple_of((g * GROUP + h) * HD, HD), HD)
                scores = lax.dot_general(
                    keys, q2[b, :, head], (((1,), (1,)), ((), ())), preferred_element_type=F32
                ) + bias[b]
                peak = jnp.max(scores, axis=0, keepdims=True)
                exponent = jnp.exp2((scores - peak) * F32(HD ** -0.5 * LOG2E))
                inverse = 1.0 / jnp.sum(exponent, axis=0, keepdims=True)
                weights = (exponent * inverse).astype(BF16)
                wts[b, g * GROUP + h] = weights
                total = total + jnp.dot(weights, do2[b, :, head], preferred_element_type=F32)
            for j in range(5):
                slots[b, j, :, lanes] = total[j * BLOCK:(j + 1) * BLOCK]

        return group

    for b in range(2):
        slots[b, 5] = jnp.zeros((BLOCK, 256), F32)

    def lay(g):
        lanes = pl.ds(g * HD, HD)

        def one(t, carry):
            place = plan_ref[0, t]
            parts = []
            for b in range(2):
                j = places[b] - place
                j = jnp.where((j >= 0) & (j <= 4), j, 5)
                parts.append(slots[b, j, :, lanes])
            dvs[g, t // 8, (t // 2) % NX, t % 2] = (parts[0] + parts[1]).astype(BF16)
            return carry

        lax.fori_loop(0, 16, one, 0)

    sides = (1 - yh, yh)
    far, close, joint, to_y, held_total = {}, {}, {}, {}, {}

    def dv_send(g, src, number, side, target):
        return send(src, dvr.at[g, number, side], ds_.at[g, number, side], dr.at[g, number, side], target)

    def dv_out(g, side):
        row = sides[side]
        far[g, side] = (
            dv_send(g, dvs.at[g, row, x2, 0], 0, side, xp_dev),
            dv_send(g, dvs.at[g, row, x2, 1], 1, side, xm_dev),
        )
        close[g, side] = (
            dv_send(g, dvs.at[g, row, xp, 1], 2, side, xp_dev),
            dv_send(g, dvs.at[g, row, xm, 0], 3, side, xm_dev),
        )

    def dv_join(g, side):
        out = []
        for way in range(2):
            far[g, side][way].wait_recv()
            mine = dvs[g, sides[side], xp, 0] if way == 0 else dvs[g, sides[side], xm, 1]
            dvt[g, way, side] = (mine.astype(F32) + dvr[g, way, side].astype(F32)).astype(BF16)
            out.append(dv_send(g, dvt.at[g, way, side], 4 + way, side, xp_dev if way == 0 else xm_dev))
        joint[g, side] = out

    def chip_total(g, side, b):
        for copy in (close[g, side][1 - b], joint[g, side][b]):
            copy.wait_recv()
        one, two = (3, 4) if b == 0 else (2, 5)
        return (
            dvs[g, sides[side], x, b].astype(F32)
            + dvr[g, one, side].astype(F32)
            + dvr[g, two, side].astype(F32)
        )

    def dv_peer(g):
        to_y[g] = []
        for b in range(2):
            vgp[g, 0, b] = chip_total(g, 0, b).astype(BF16)
            to_y[g].append(send(vgp.at[g, 0, b], vgp.at[g, 1, b], dys.at[g, b], dyr.at[g, b], y4_dev))

    def dv_own(g):
        held_total[g] = [chip_total(g, 1, b) for b in range(2)]

    def dv_final(g):
        out = []
        for b in range(2):
            to_y[g][b].wait_recv()
            out.append((held_total[g][b] + vgp[g, 1, b].astype(F32)).astype(BF16))
        return out

    weigh(0)(0)
    weigh(1)(0)
    lay(0)
    dv_out(0, 0)
    gather_peer_forward(*keys_of[1])
    dv_join(0, 0)
    dv_out(0, 1)
    key_local[1].wait()
    key_core[1].wait_recv()
    gather_done(*keys_of[1])
    ring_step(4)
    weigh(0)(1)
    weigh(1)(1)
    lay(1)
    dv_out(1, 0)
    dv_peer(0)
    dv_join(0, 1)
    dv_join(1, 0)
    dv_out(1, 1)
    ring_step(5)
    dv_own(0)
    dv_peer(1)
    dv_join(1, 1)
    ring_step(6)

    def product_of(part, value_grad):
        for j in range(6):
            lanes = pl.ds(j * 384, 384)
            product = jnp.zeros((384, HD), F32)
            for b in range(2):
                product = product + lax.dot_general(
                    tok2[b, :, lanes], value_grad[b], (((0,), (0,)), ((), ())), preferred_element_type=F32
                )
            gb[part, pl.ds(j * 384, 384), :] = product

    ends = (pl.ds(0, 288), pl.ds(288, 288))

    def regroup(part):
        for j in range(NZ):
            for a in range(NYL):
                for h in range(2):
                    for k in range(NX):
                        to = (h * NYL + a) * 72 + j * 6
                        xb[part, k, pl.ds(to, 6), :] = gb[part, pl.ds(j * 192 + (a * 2 + h) * 24 + k * 6, 6), :]
        for k in range(NX):
            xbs[part, k] = xb[part, k].astype(BF16)

    def g_send(part, src, number, target):
        return send(src, xbr.at[part, number], bs.at[part, number], br.at[part, number], target)

    def g_far(part):
        return [
            g_send(part, xbs.at[part, x2, ends[0]], 0, xp_dev),
            g_send(part, xbs.at[part, x2, ends[1]], 1, xm_dev),
        ]

    def g_close(part):
        return [
            g_send(part, xbs.at[part, xp, ends[1]], 2, xp_dev),
            g_send(part, xbs.at[part, xm, ends[0]], 3, xm_dev),
        ]

    def g_join(part, copies):
        out = []
        for way, at, target in ((0, xp, xp_dev), (1, xm, xm_dev)):
            copies[way].wait_recv()
            xbt[part, way] = (xb[part, at, ends[way], :] + xbr[part, way].astype(F32)).astype(BF16)
            out.append(g_send(part, xbt.at[part, way], 4 + way, target))
        return out

    def g_total(part, close_pair, joint_pair):
        for end, one, two in ((0, 3, 4), (1, 2, 5)):
            close_pair[1 - end].wait_recv()
            joint_pair[end].wait_recv()
            yb[part, ends[end], :] = (
                xb[part, x, ends[end], :] + xbr[part, one].astype(F32) + xbr[part, two].astype(F32)
            )
        for k in range(NY):
            ybs[part, k] = yb[part, pl.ds(k * 72, 72), :].astype(BF16)
        out = []
        for d in (4, 3, 5, 2, 6, 1, 7):
            there = (y + d) % NY
            out.append(
                send(ybs.at[part, there], ybr.at[part, d], bys.at[part, d], byr.at[part, d], dev(z, there, x, c))
            )
        return out

    lt.wait()
    et.wait_recv()
    value_grad = dv_final(0)
    product_of(0, value_grad)
    regroup(0)
    far0 = g_far(0)
    close0 = g_close(0)
    dv_own(1)
    lw.wait()
    for i in range(NYL):
        ring_plus(6, i).wait_recv()
    weight = wbuf[...].reshape(48 * 48, 256)
    for b in range(2):
        vall[2 * chip + b] = jnp.dot(tok2[b], weight, preferred_element_type=F32).astype(BF16)
    gather_y(vall, vs, vr)
    joint0 = g_join(0, far0)
    value_grad = dv_final(1)
    product_of(1, value_grad)
    regroup(1)
    far1 = g_far(1)
    close1 = g_close(1)

    y0 = g_total(0, close0, joint0)
    joint1 = g_join(1, far1)
    gather_x(vall, vs, vr)
    y1 = g_total(1, close1, joint1)
    gather_peer(vall, vs, vr)
    gather_x_forward(vall, vs, vr)
    gather_peer_forward(vall, vs, vr)
    for part, copies in ((0, y0), (1, y1)):
        for copy in copies:
            copy.wait_recv()
        total = yb[part, pl.ds(pl.multiple_of(y * 72, 8), 72), :]
        for d in range(1, NY):
            total = total + ybr[part, d].astype(F32)
        bsum[part] = total

    zs[...] = jnp.zeros((NZ, 2, 8, HD), F32)
    for j in range(NZ):
        for core in range(2):
            at = pl.ds(j * 6 + core * 3, 3)
            zs[j, core, 0:3, :] = bsum[0, at, :]
            zs[j, core, 3:6, :] = bsum[1, at, :]

    z_copies = []
    for d in (6, 5, 7, 4, 8, 3, 9, 2, 10, 1, 11, 0):
        there = (z + d) % NZ
        if d > 0:
            z_copies.append(
                send(zs.at[there, c], zr.at[0, d], zss.at[0, d], zrs.at[0, d], dev(there, y, x, c))
            )
        z_copies.append(
            send(zs.at[there, 1 - c], zr.at[1, d], zss.at[1, d], zrs.at[1, d], dev(there, y, x, 1 - c))
        )

    gather_done(vall, vs, vr)

    def attend(b, g):
        held = jnp.concatenate([vall[at, :, pl.ds(g * HD, HD)] for at in key_at[b]], axis=0)
        for h in range(g * GROUP, g * GROUP + GROUP):
            flipped = lax.dot_general(
                held, wts[b, h], (((0,), (0,)), ((), ())), preferred_element_type=F32
            )
            att2[b, :, pl.ds(h * HD, HD)] = flipped.T.astype(BF16)

    att_local, att_core = [], []
    for g in range(2):
        attend(0, g)
        attend(1, g)
        part = pl.ds(g * 512, 512)
        there = pl.ds(pl.multiple_of(c * 1024 + g * 512, 512), 512)
        att_core.append(
            send(att2.at[1 - c, :, part], att_out.at[:, there], es.at[(4, 7)[g]], er.at[(4, 7)[g]], core_dev)
        )
        copy = pltpu.make_async_copy(att2.at[c, :, part], att_out.at[:, there], lsem.at[(5, 8)[g]])
        copy.start()
        att_local.append(copy)
    for copy in z_copies:
        copy.wait_recv()
    mine, theirs = zs[z, c], zr[1, 0]
    for d in range(1, NZ):
        mine = mine + zr[0, d]
        theirs = theirs + zr[1, d]
    low, high = jnp.where(c == 0, mine, theirs), jnp.where(c == 0, theirs, mine)
    wg_out[:, 0:128] = low[0:3]
    wg_out[:, 128:256] = low[3:6]
    wg_out[:, 256:384] = high[0:3]
    wg_out[:, 384:512] = high[3:6]
    for copy in att_local:
        copy.wait()
    for copy in att_core:
        copy.wait_recv()
    for copy in started:
        copy.wait_send()


def shards(tokens, queries, key_rows, out_grad, value_weight, documents, block_plan):
    anywhere = pl.BlockSpec(memory_space=pl.ANY)
    in_vmem = pl.BlockSpec(memory_space=pltpu.VMEM)
    dma = pltpu.SemaphoreType.DMA
    vmem = pltpu.VMEM
    attended, weight_grad = pl.pallas_call(
        body,
        out_shape=(
            jax.ShapeDtypeStruct((BLOCK, 2048), BF16),
            jax.ShapeDtypeStruct((3, 512), F32),
        ),
        in_specs=[anywhere] * 5 + [in_vmem, pl.BlockSpec(memory_space=pltpu.SMEM)],
        out_specs=(anywhere, in_vmem),
        scratch_shapes=[
            vmem((2, BLOCK, 2304), BF16),
            vmem((2, BLOCK, 1024), BF16),
            vmem((2, BLOCK, 1024), BF16),
            vmem((16, BLOCK, HD), BF16),
            vmem((16, BLOCK, HD), BF16),
            vmem((16, BLOCK, 256), BF16),
            vmem((48, 48, 256), BF16),
            vmem((2, 5 * BLOCK, BLOCK), F32),
            vmem((2, 8, 5 * BLOCK, BLOCK), BF16),
            vmem((2, 6, BLOCK, 256), F32),
            vmem((2, 2, NX, 2, BLOCK, HD), BF16),
            vmem((2, 6, 2, BLOCK, HD), BF16),
            vmem((2, 2, 2, BLOCK, HD), BF16),
            vmem((2, 2, 2, BLOCK, HD), BF16),
            vmem((2, BLOCK, 1024), BF16),
            vmem((2, 2304, HD), F32),
            vmem((2, NX, 576, HD), F32),
            vmem((2, NX, 576, HD), BF16),
            vmem((2, 6, 288, HD), BF16),
            vmem((2, 2, 288, HD), BF16),
            vmem((2, 576, HD), F32),
            vmem((2, NY, 72, HD), BF16),
            vmem((2, NY, 72, HD), BF16),
            vmem((2, 72, HD), F32),
            vmem((NZ, 2, 8, HD), F32),
            vmem((2, NZ, 8, HD), F32),
            dma((9,)),
            dma((8,)), dma((8,)),
            dma((4,)), dma((4,)),
            dma((2, 6, 4)), dma((2, 6, 4)),
            dma((2, 7, 2)), dma((2, 7, 2)),
            dma((7, 2)), dma((7, 2)),
            dma((2, 6, 2)), dma((2, 6, 2)),
            dma((2, 2)), dma((2, 2)),
            dma((2, 6)), dma((2, 6)),
            dma((2, NY)), dma((2, NY)),
            dma((2, NZ)), dma((2, NZ)),
        ],
        compiler_params=pltpu.CompilerParams(
            collective_id=0, has_side_effects=True, vmem_limit_bytes=60 * 1024 * 1024
        ),
        name="value_path",
    )(
        tokens[0], queries[0], key_rows[0], out_grad[0], value_weight,
        documents.reshape(16, BLOCK), block_plan,
    )
    return attended[None], weight_grad


def solution(mesh):
    in_specs = (
        P("fsdp", "seq", None),
        P("fsdp", "seq", None),
        P("fsdp", "seq", None),
        P("fsdp", "seq", None),
        P("fsdp", None),
        P("fsdp", None),
        P("fsdp", None),
    )
    out_specs = (P("fsdp", "seq", None), P(("fsdp", "seq"), None))
    return jax.shard_map(shards, mesh=mesh, in_specs=in_specs, out_specs=out_specs, check_vma=False)
```
